256 devices in a mesh: period: 128 (over z, x, y), half: 2 (over core).
Axes of the slice: x: 4, y: 4, z: 8, core: 2. Of those that a mesh axis runs over, the one named last changes fastest.
Arguments:
- probes: float32 [1024, 4, 512], P('period', None, 'half'), may hold values from -6 to 6
- footprints: bfloat16 [1024, 512, 512], P('period', None, 'half'), may hold values from -0.25 to 0.25
- lag_weights: float32 [1024, 4], P('period'), may hold values from 0.2 to 2
- owners: int32 [1024, 4], P('period'), may hold values from 0 to 127, all different within a row; in each aligned block of 8 rows (0 to 7, 8 to 15, ...) at most 2 rows name the same one
- window_tiles: int32 [1024, 2], P('period', 'half'), may hold values from 0 to 10
- coords: int32 [2, 3072], replicated, may hold values from 0 to 63
- temporal: float32 [128, 128], replicated, as said below
Outputs:
- coefficients: float32 [4, 4], replicated
- residual: float32 [1024, 4, 512], P('period', None, 'half')
The draws below stay inside these ranges and needn't reach their ends.
Inputs may be any that keep to these rules, and one draw needn't show every extreme that they name: `owners`: each row names 4 different periods. Among the 8 rows of one index of period, no period is named more than 2 times, and one is named exactly 2 times. `temporal`: symmetric.
All inputs are finite; a program needn't handle non-finite values.
Results may differ from the reference program's by a relative error of at most 0.025.
Values may be sent and summed in bfloat16 or wider, within the bound.
No kernel may reach another device: no remote copies, remote signals or barrier semaphores. Data moves between devices by JAX's collectives and lax.ppermute only.
A program may use at most 64 MiB of HBM per device.

```python
import math
import jax
import jax.numpy as jnp
import numpy as np
from jax import lax

CELLS = 3072
WIN = 256
SOUND = 512
TOP = 4
GRID = 64
PROBES = 4
BLK_DEV = 8
PERIODS = 128
BLOCKS = 1024
CAP = 2
N_PERIOD = 128


def draw_temporal(key, part):
    key_sym, key_diag = jax.random.split(jax.random.fold_in(key, 17))
    raw = jax.random.normal(key_sym, (PERIODS, PERIODS), jnp.float32)
    symmetric = (raw + raw.T) * (0.6 / jnp.sqrt(2.0 * PERIODS))
    diagonal = jax.random.uniform(key_diag, (PERIODS,), jnp.float32, minval=0.5, maxval=1.5)
    return symmetric + jnp.diag(diagonal)


def set_ends(result, rng, low, top_value):
    extent = result.shape
    place = [jax.random.randint(jax.random.fold_in(rng, axis), (), 0, extent[axis]) for axis in range(len(extent))]
    result = result.at[tuple(place)].set(low)
    longest = extent.index(max(extent))
    place[longest] = (place[longest] + 1) % extent[longest]
    return result.at[tuple(place)].set(top_value)


def level_of(key, dims, cuts, least, high):
    loudness, own = 1.0, jax.random.fold_in(key, 6)
    for position, shards_of in cuts:
        heights = jnp.exp(jax.random.uniform(jax.random.fold_in(own, position), (shards_of,), jnp.float32, least / len(cuts), high / len(cuts)))
        loudness = loudness * jnp.repeat(heights, dims[position] // shards_of).reshape([-1 if axis == position else 1 for axis in range(len(dims))])
    return loudness


def assign_block(rng, own, number, rows, amount, top, bound, skew):
    ranking = jax.random.permutation(rng, amount)
    crowded, common = load_shares(amount, rows * top, bound, skew, True), load_shares(amount, rows * top, bound, skew, False)
    places = jnp.arange(amount)

    def named(lengths, rotation):
        used = int((lengths > 0).sum())
        fixed = max(1, used // 4)
        shifted = fixed + (places - fixed + rotation * (used - fixed)) % max(1, amount - fixed)
        return jnp.zeros((amount,), jnp.int32).at[ranking[jnp.where(places < fixed, places, shifted)]].set(jnp.asarray(lengths, jnp.int32))

    lengths = jnp.where(number % 4 == 0, named(crowded, number // 4), named(common, number - number // 4 - 1))
    mixed = jax.random.permutation(jax.random.fold_in(own, 3), amount)
    source_of, receiver = mixed[0:amount // 2 * 2:2], mixed[1:amount // 2 * 2:2]
    slack = jnp.minimum(lengths[source_of] - 1, bound - lengths[receiver]) // 2
    slack = jnp.where((source_of == ranking[0]) | (receiver == ranking[0]) | (lengths[receiver] == 0), 0, jnp.maximum(slack, 0))
    shifted = jax.random.randint(jax.random.fold_in(own, 4), (amount // 2,), 0, 1 << 20) % (slack + 1)
    lengths = lengths.at[source_of].add(-shifted).at[receiver].add(shifted)
    items = jnp.searchsorted(jnp.cumsum(lengths), jnp.arange(rows * top), side="right").astype(jnp.int32)
    grid = items.reshape(top, rows).T
    grid = grid[jax.random.permutation(jax.random.fold_in(own, 1), rows)]
    rotation = jax.random.randint(jax.random.fold_in(own, 2), (rows, 1), 0, top)
    return jnp.take_along_axis(grid, (jnp.arange(top)[None, :] + rotation) % top, axis=1)


def load_shares(number_of, total, limit, slope, full):
    portions = [(1 << 20) // math.isqrt(standing ** slope) + 1 for standing in range(1, number_of + 1)]
    largest = limit if full else min(limit, max(-(-total // number_of), total * portions[0] // sum(portions)))
    least = 1 if total - largest >= number_of - 1 else 0
    given, rest = [largest] + [least] * (number_of - 1), total - largest - least * (number_of - 1)
    while rest > 0:
        candidates = [i for i in range(1, number_of) if given[i] < largest] or [i for i in range(1, number_of) if given[i] < limit]
        mass, left = sum([portions[i] for i in candidates]), rest
        for i in candidates:
            addition = min(limit - given[i], max(1, left * portions[i] // mass), rest)
            given[i] = given[i] + addition
            rest = rest - addition
    return np.array(given)


def noise(key, dims, width, reach, cuts=(), held_as=jnp.bfloat16):
    values = jax.random.normal(key, dims, jnp.float32) * width
    if len(cuts) > 0:
        values = level_of(key, dims, cuts, -0.22, 0.18) * values
    return jnp.clip(values, min=-reach, max=reach).astype(held_as)


def setup_inputs(seed: int = 0) -> dict:
    keys = jax.random.split(jax.random.key(seed), 8)
    probes = noise(keys[0], (BLOCKS, PROBES, SOUND), 1.0, 6.0, ((0, 128), (2, 2)), jnp.float32)
    footprints = noise(keys[1], (BLOCKS, SOUND, 2 * WIN), (2 * WIN) ** -0.5, 0.25, ((0, 128), (2, 2)))
    lag_weights = jnp.clip(jnp.exp(math.log(2.0) - 2.3025851 * jax.random.uniform(keys[2], (BLOCKS, TOP), jnp.float32) ** level_of(keys[2], (BLOCKS, TOP), ((0, 128),), -0.2, 0.2)), 0.2, 2.0)
    owners_keys = jax.random.split(jax.random.fold_in(keys[3], 1), BLOCKS // BLK_DEV)
    owners_turns = jax.random.permutation(jax.random.fold_in(keys[3], 3), BLOCKS // BLK_DEV)
    owners = jax.vmap(lambda own, number: assign_block(jax.random.fold_in(keys[3], 2), own, number, BLK_DEV, N_PERIOD, TOP, CAP, 2))(owners_keys, owners_turns).reshape((BLOCKS, TOP))
    window_tiles = set_ends(jax.random.randint(keys[4], (BLOCKS, 2), 0, CELLS // 256 - WIN // 128 + 1), jax.random.fold_in(keys[4], 1), 0, (CELLS // 256 - WIN // 128 + 1) - 1).astype(jnp.int32)
    coords = set_ends(jax.random.randint(keys[5], (2, CELLS), 0, GRID), jax.random.fold_in(keys[5], 1), 0, GRID - 1).astype(jnp.int32)
    temporal = draw_temporal(jax.random.fold_in(keys[7], 71), 0)
    return dict(probes=probes, footprints=footprints, lag_weights=lag_weights, owners=owners, window_tiles=window_tiles, coords=coords, temporal=temporal)


epsilon = 1e-06
kernel_scale = 0.05
kernel_length = 6.0
highest = lax.Precision.HIGHEST

def spatial_kernel(coords):
    delta_x = coords[0][:, None] - coords[0][None, :]
    delta_y = coords[1][:, None] - coords[1][None, :]
    squared = (delta_x * delta_x + delta_y * delta_y).astype(jnp.float32)
    return kernel_scale * jnp.exp(-jnp.sqrt(squared) / kernel_length)

def window_cells(window_tiles):
    half_cells = CELLS // 2
    offsets = jnp.arange(WIN, dtype=jnp.int32)
    first_half = window_tiles[:, 0:1] * 128 + offsets[None, :]
    second_half = half_cells + window_tiles[:, 1:2] * 128 + offsets[None, :]
    return jnp.concatenate([first_half, second_half], axis=1).astype(jnp.int32)

def apply_operator(vector, footprints, lag_weights, owners, cells, kernel, temporal):
    vector_low = vector.astype(jnp.bfloat16).reshape(N_PERIOD, BLK_DEV, PROBES, SOUND)
    foot_blocks = footprints.reshape(N_PERIOD, BLK_DEV, SOUND, 2 * WIN)
    weight_blocks = lag_weights.reshape(N_PERIOD, BLK_DEV, TOP)
    owner_blocks = owners.reshape(N_PERIOD, BLK_DEV, TOP)
    cell_blocks = cells.reshape(N_PERIOD, BLK_DEV, 2 * WIN)
    probe_index = jnp.arange(PROBES, dtype=jnp.int32)[None, None, :, None]

    def adjoint_group(flux, members):
        low_group, foot_group, weight_group, owner_group, cell_group = members
        partial_value = jnp.einsum('bps,bsw->bpw', low_group.astype(jnp.float32), foot_group.astype(jnp.float32))
        terms = weight_group[:, :, None, None] * partial_value[:, None, :, :]
        flux = flux.at[owner_group[:, :, None, None], probe_index, cell_group[:, None, None, :]].add(terms)
        return (flux, None)
    flux_start = jnp.zeros((N_PERIOD, PROBES, CELLS), jnp.float32)
    flux, unused = lax.scan(adjoint_group, flux_start, (vector_low, foot_blocks, weight_blocks, owner_blocks, cell_blocks))
    spatial = jnp.einsum('npc,rc->npr', flux, kernel, precision=highest)
    field = jnp.einsum('tn,npr->tpr', temporal, spatial, precision=highest).astype(jnp.bfloat16)

    def forward_group(carry, members):
        foot_group, weight_group, owner_group, cell_group = members
        windows = field[owner_group[:, :, None, None], probe_index, cell_group[:, None, None, :]]
        sounded = jnp.einsum('bk,bkpw,bsw->bps', weight_group, windows.astype(jnp.float32), foot_group.astype(jnp.float32))
        return (carry, sounded)
    carry, images = lax.scan(forward_group, jnp.zeros((), jnp.float32), (foot_blocks, weight_blocks, owner_blocks, cell_blocks))
    return images.reshape(BLOCKS, PROBES, SOUND)

def reference(probes, footprints, lag_weights, owners, window_tiles, coords, temporal):
    kernel = spatial_kernel(coords)
    cells = window_cells(window_tiles)
    total_rows = float(BLOCKS * SOUND)

    def mean_of(values):
        return lax.optimization_barrier(jnp.sum(values, axis=(0, 2))) / total_rows
    start_scale = jnp.sqrt(mean_of(probes * probes) + epsilon)
    first_q = probes / start_scale[None, :, None]
    image_one = apply_operator(first_q, footprints, lag_weights, owners, cells, kernel, temporal)
    alpha_one = mean_of(first_q * image_one)
    rest_one = image_one - alpha_one[None, :, None] * first_q
    beta_one = jnp.sqrt(mean_of(rest_one * rest_one) + epsilon)
    second_q = rest_one / beta_one[None, :, None]
    image_two = apply_operator(second_q, footprints, lag_weights, owners, cells, kernel, temporal)
    image_two = image_two - beta_one[None, :, None] * first_q
    alpha_two = mean_of(second_q * image_two)
    residual = image_two - alpha_two[None, :, None] * second_q
    beta_two = jnp.sqrt(mean_of(residual * residual) + epsilon)
    coefficients = jnp.stack([alpha_one, beta_one, alpha_two, beta_two], axis=0)
    return (coefficients, residual)
```

```python
import jax
import jax.numpy as jnp
from jax import lax
from jax.sharding import PartitionSpec as P

epsilon = 1e-06
kernel_scale = 0.05
kernel_length = 6.0
highest = lax.Precision.HIGHEST


def permuted(value, axis, target_of):
    count = lax.axis_size(axis)
    return lax.ppermute(value, axis, [(source, target_of(source)) for source in range(count)])


def from_other_half(value):
    return permuted(value, "half", lambda source: 1 - source)


def total_sum(value):
    count = lax.axis_size("period")
    value = (value + from_other_half(value)).reshape(1, -1)
    everyone = lax.all_to_all(
        jnp.broadcast_to(value, (count, value.shape[1])),
        "period",
        split_axis=0,
        concat_axis=0,
        tiled=True,
    )
    return jnp.sum(everyone, axis=0)


def split_parts(value, count):
    parts = []
    for _ in range(count):
        part = lax.reduce_precision(value, 8, 7)
        parts.append(part.astype(jnp.bfloat16))
        value = value - part
    return parts


def body(probes, footprints, lag_weights, owners, window_tiles, coords, temporal):
    periods = lax.axis_size("period")
    half_index = lax.axis_index("half")
    block_count, top_count = owners.shape
    probe_count = probes.shape[1]
    half_sound = probes.shape[2]
    sound_count = footprints.shape[1]
    window = footprints.shape[2]
    win_tiles = window // 128
    cell_count = coords.shape[1]
    half_cells = cell_count // 2
    tile_count = half_cells // 128
    total_rows = float(block_count * periods * sound_count)
    row_count = block_count * probe_count

    own_tiles = window_tiles[:, 0]
    other_tiles = from_other_half(own_tiles)

    def tile_hot(tiles):
        return (
            tiles[:, None, None] + jnp.arange(win_tiles, dtype=jnp.int32)[None, :, None]
            == jnp.arange(tile_count, dtype=jnp.int32)[None, None, :]
        ).astype(jnp.float32)

    own_hot, other_hot = tile_hot(own_tiles), tile_hot(other_tiles)
    own_coords = lax.dynamic_slice_in_dim(coords, half_index * half_cells, half_cells, 1)
    other_coords = lax.dynamic_slice_in_dim(coords, (1 - half_index) * half_cells, half_cells, 1)
    order_coords = jnp.concatenate([own_coords, other_coords], axis=1)
    delta_x = order_coords[0][:, None] - own_coords[0][None, :]
    delta_y = order_coords[1][:, None] - own_coords[1][None, :]
    squared = (delta_x * delta_x + delta_y * delta_y).astype(jnp.float32)
    kernel = (kernel_scale * jnp.exp(-jnp.sqrt(squared) / kernel_length)).astype(jnp.bfloat16)

    def exchange(value):
        return lax.all_to_all(value, "period", split_axis=0, concat_axis=0, tiled=True)

    def place(piece, hot):
        tiles = piece.reshape(block_count, probe_count, win_tiles, 128)
        return jnp.einsum("bjt,bpjl->bptl", hot, tiles, precision=highest).reshape(
            row_count, half_cells
        )

    def spatial_part(vector):
        piece = jnp.einsum(
            "bps,bsw->bpw",
            vector.astype(jnp.bfloat16),
            footprints,
            preferred_element_type=jnp.float32,
        )
        dense = jnp.concatenate(
            [place(piece, own_hot), place(from_other_half(piece), other_hot)], axis=1
        )
        both = jnp.concatenate(split_parts(dense, 2), axis=0)
        spread = jnp.dot(both, kernel, preferred_element_type=jnp.float32)
        spread = spread[:row_count] + spread[row_count:]
        spread = spread.reshape(row_count, tile_count, 128)
        return jnp.transpose(spread, (2, 1, 0)).reshape(128, tile_count * row_count)

    def mix_periods(received, choice):
        received = received.reshape(periods, tile_count, block_count, probe_count)
        gathered = jnp.einsum(
            "sbn,stbp->ntp", choice, received.astype(jnp.float32), precision=highest
        )
        mixed = jnp.einsum("mn,ntp->mtp", temporal, gathered, precision=highest)
        return jnp.einsum("dbn,ntp->dtbp", choice, mixed, precision=highest).reshape(
            periods, tile_count * row_count
        )

    def sounded_part(field):
        field = field.reshape(128, tile_count, block_count, probe_count).astype(jnp.float32)
        windows = jnp.einsum("bjt,gtbp->bpjg", own_hot, field, precision=highest)
        windows = windows.astype(jnp.bfloat16).reshape(block_count, probe_count, window)
        partial_sound = jnp.einsum(
            "bpw,bsw->bps", windows, footprints, preferred_element_type=jnp.float32
        )
        return partial_sound + from_other_half(partial_sound)

    lag_parts = split_parts(lag_weights.reshape(-1), 3)
    table = jnp.concatenate([owners.reshape(-1).astype(jnp.bfloat16)] + lag_parts)
    table_rows = jnp.broadcast_to(table[None, :], (periods, table.shape[0]))

    whole_probes = lax.all_gather(probes.astype(jnp.bfloat16), "half", axis=2, tiled=True)
    spread_one = spatial_part(whole_probes).astype(jnp.bfloat16)
    wide = exchange(jnp.concatenate([spread_one, table_rows], axis=1))
    received_one = wide[:, : tile_count * row_count]
    tables = wide[:, tile_count * row_count :].astype(jnp.float32)
    tables = tables.reshape(periods, 4, block_count, top_count)
    all_owners = tables[:, 0].astype(jnp.int32)
    all_weights = tables[:, 1] + tables[:, 2] + tables[:, 3]
    choice = jnp.sum(
        jnp.where(
            all_owners[:, :, :, None] == jnp.arange(periods, dtype=jnp.int32),
            all_weights[:, :, :, None],
            0.0,
        ),
        axis=2,
    )
    image_one = sounded_part(exchange(mix_periods(received_one, choice).astype(jnp.bfloat16)))
    received_two = exchange(spatial_part(image_one).astype(jnp.bfloat16))
    image_two = sounded_part(exchange(mix_periods(received_two, choice).astype(jnp.bfloat16)))

    first = lax.dynamic_slice_in_dim(image_one, half_index * half_sound, half_sound, 2)
    second = lax.dynamic_slice_in_dim(image_two, half_index * half_sound, half_sound, 2)

    def inner(left, right):
        return jnp.sum(left * right, axis=(0, 2))

    sums = jnp.stack(
        [
            inner(probes, probes),
            inner(probes, first),
            inner(first, first),
            inner(probes, second),
            inner(first, second),
            inner(second, second),
        ]
    )
    pp, pw, ww, px, wx, xx = total_sum(sums).reshape(sums.shape) / total_rows
    scale_square = pp + epsilon
    scale = jnp.sqrt(scale_square)
    alpha_one = pw / scale_square
    rest = (ww - 2.0 * alpha_one * pw + alpha_one * alpha_one * pp) / scale_square
    beta_one = jnp.sqrt(jnp.maximum(rest, 0.0) + epsilon)
    cross = wx - alpha_one * ww - alpha_one * px + alpha_one * alpha_one * pw
    alpha_two = (cross / (beta_one * beta_one) - (pw - alpha_one * pp)) / scale_square
    of_second = 1.0 / (scale * beta_one)
    of_first = -(alpha_one + alpha_two) * of_second
    of_probes = (alpha_one * alpha_two / beta_one - beta_one) / scale
    square = (
        of_second * of_second * xx
        + of_first * of_first * ww
        + of_probes * of_probes * pp
        + 2.0 * (of_second * of_first * wx + of_second * of_probes * px + of_first * of_probes * pw)
    )
    beta_two = jnp.sqrt(jnp.maximum(square, 0.0) + epsilon)
    residual = (
        of_second[None, :, None] * second
        + of_first[None, :, None] * first
        + of_probes[None, :, None] * probes
    )
    coefficients = jnp.stack([alpha_one, beta_one, alpha_two, beta_two], axis=0)
    return (coefficients, residual)


def solution(mesh):
    in_specs = (
        P("period", None, "half"),
        P("period", None, "half"),
        P("period", None),
        P("period", None),
        P("period", "half"),
        P(),
        P(),
    )
    out_specs = (P(), P("period", None, "half"))
    return jax.shard_map(body, mesh=mesh, in_specs=in_specs, out_specs=out_specs, check_vma=False)
```

```python
import functools

import jax
import jax.numpy as jnp
from jax import lax
from jax.experimental import pallas as pl
from jax.experimental.pallas import tpu as pltpu
from jax.sharding import PartitionSpec as P

epsilon = 1e-06
kernel_scale = 0.05
kernel_length = 6.0
log2e = 1.4426950408889634
log2_scale = -4.321928094887363
LANES = 128
HALF_LANES = 64


vmem = pl.BlockSpec(memory_space=pltpu.VMEM)
smem = pl.BlockSpec(memory_space=pltpu.SMEM)


def from_other_half(value):
    return lax.ppermute(value, "half", [(0, 1), (1, 0)])


def exchange(value):
    return lax.all_to_all(value, "period", split_axis=0, concat_axis=0, tiled=True)


def block_of_row(shape, block_count):
    return lax.rem(lax.broadcasted_iota(jnp.int32, shape, 0), block_count)


def halves(value):
    high = value.astype(jnp.bfloat16)
    low = (value - high.astype(jnp.float32)).astype(jnp.bfloat16)
    return high, low


def dot(left, right, dims=((1,), (0,))):
    return lax.dot_general(left, right, (dims, ((), ())), preferred_element_type=jnp.float32)


def send_adjoint(vector, tiles_ref, feet_ref, table_ref, out_ref, placed):
    block_count = feet_ref.shape[0]
    rows = vector.shape[0]
    window = feet_ref.shape[2]
    piece_block = block_of_row((rows, window), block_count)
    placed[...] = jnp.zeros_like(placed)
    for block in range(block_count):
        piece = dot(vector, feet_ref[block])
        start = pl.multiple_of(tiles_ref[block, 0] * LANES, LANES)
        old = placed[:, pl.ds(start, window)]
        placed[:, pl.ds(start, window)] = jnp.where(piece_block == block, piece, old)
    table = table_ref[...]
    lane = lax.broadcasted_iota(jnp.int32, table.shape, 1)
    probe_count = rows // block_count
    tile_count = placed.shape[1] // LANES
    for tile in range(tile_count):
        for probe in range(probe_count):
            values = placed[
                probe * block_count : (probe + 1) * block_count, tile * LANES : (tile + 1) * LANES
            ]
            first = jnp.where(lane < HALF_LANES, values, table)
            second = jnp.where(lane < HALF_LANES, pltpu.roll(values, HALF_LANES, 1), table)
            at = (tile * probe_count + probe) * 2 * block_count
            out_ref[at : at + 2 * block_count, :] = jnp.concatenate(
                [first, second], axis=0
            ).astype(jnp.bfloat16)
    used = tile_count * probe_count * 2 * block_count
    out_ref[used:, :] = jnp.zeros((out_ref.shape[0] - used, LANES), jnp.bfloat16)


def start_kernel(half_ref, tiles_ref, own_ref, other_ref, feet_ref, table_ref, out_ref, probes_ref, placed):
    half = half_ref[0]
    block_count, probe_count, half_sound = own_ref.shape
    own_at = pl.multiple_of(half * half_sound, LANES)
    other_at = pl.multiple_of((1 - half) * half_sound, LANES)
    for probe in range(probe_count):
        rows = slice(probe * block_count, (probe + 1) * block_count)
        probes_ref[rows, pl.ds(own_at, half_sound)] = own_ref[:, probe, :]
        probes_ref[rows, pl.ds(other_at, half_sound)] = other_ref[:, probe, :]
    vector = probes_ref[...].astype(jnp.bfloat16)
    send_adjoint(vector, tiles_ref, feet_ref, table_ref, out_ref, placed)


def spatial_build_kernel(left_ref, right_ref, out_ref):
    squared = dot(left_ref[...], right_ref[...], ((0,), (0,)))
    squared = jnp.maximum(squared, 1e-12)
    distance = squared * lax.rsqrt(squared)
    out_ref[...] = jnp.exp2(distance * (-log2e / kernel_length) + log2_scale).astype(jnp.bfloat16)


def mix(received, choice, temporal):
    periods = temporal.shape[0]
    both = dot(choice, received, ((0,), (0,)))
    gathered = both[:periods] + both[periods:]
    mixed = lax.dot_general(
        temporal,
        gathered,
        (((1,), (0,)), ((), ())),
        precision=lax.Precision.HIGHEST,
        preferred_element_type=jnp.float32,
    )
    high, low = halves(mixed)
    spread = dot(choice, jnp.concatenate([high, high], axis=0))
    return (spread + dot(choice[:, :periods], low)).astype(jnp.bfloat16)


def first_mix_kernel(top_count, received_ref, temporal_ref, out_ref, choice_ref):
    periods = temporal_ref.shape[0]
    received = received_ref[...]
    wide = received.astype(jnp.float32)
    lane = lax.broadcasted_iota(jnp.int32, (wide.shape[0], periods), 1).astype(jnp.float32)
    choice = jnp.zeros((wide.shape[0], periods), jnp.float32)
    for top in range(top_count):
        at = HALF_LANES + top
        owner = wide[:, at : at + 1]
        weight = (
            wide[:, at + top_count : at + top_count + 1]
            + wide[:, at + 2 * top_count : at + 2 * top_count + 1]
            + wide[:, at + 3 * top_count : at + 3 * top_count + 1]
        )
        choice = choice + jnp.where(owner == lane, weight, 0.0)
    high, low = halves(choice)
    choice_ref[...] = jnp.concatenate([high, low], axis=1)
    out_ref[...] = mix(received, choice_ref[...], temporal_ref[...])


def mix_kernel(received_ref, temporal_ref, choice_ref, out_ref):
    out_ref[...] = mix(received_ref[...], choice_ref[...], temporal_ref[...])


def spatial_kernel(block_count, tiles_ref, others_ref, received_ref, spatial_ref, out_ref, field, total):
    step = pl.program_id(0)
    rows, half_cells = field.shape
    tile_count = half_cells // LANES
    probe_count = rows // block_count

    @pl.when(step == 0)
    def _():
        lane = lax.broadcasted_iota(jnp.int32, (block_count, LANES), 1)
        for tile in range(tile_count):
            for probe in range(probe_count):
                at = (tile * probe_count + probe) * 2 * block_count
                both = received_ref[at : at + 2 * block_count, :].astype(jnp.float32)
                joined = jnp.where(
                    lane < HALF_LANES,
                    both[:block_count],
                    pltpu.roll(both[block_count:], HALF_LANES, 1),
                )
                field[
                    probe * block_count : (probe + 1) * block_count,
                    tile * LANES : (tile + 1) * LANES,
                ] = joined
        total[...] = jnp.zeros_like(total)

    depth = spatial_ref.shape[0]
    part = field[:, pl.ds(pl.multiple_of(step * depth, LANES), depth)].astype(jnp.bfloat16)
    total[...] += dot(part, spatial_ref[...])

    @pl.when(step == pl.num_programs(0) - 1)
    def _():
        window = out_ref.shape[1] // 2
        block_index = block_of_row((rows, window), block_count)
        own = jnp.zeros((rows, window), jnp.float32)
        other = jnp.zeros((rows, window), jnp.float32)
        for block in range(block_count):
            own_at = pl.multiple_of(tiles_ref[block, 0] * LANES, LANES)
            other_at = pl.multiple_of(half_cells + others_ref[block, 0] * LANES, LANES)
            own = jnp.where(block_index == block, total[:, pl.ds(own_at, window)], own)
            other = jnp.where(block_index == block, total[:, pl.ds(other_at, window)], other)
        out_ref[:, :window] = own
        out_ref[:, window:] = other


def sound(mine_ref, theirs_ref, feet_ref, other_feet_ref):
    block_count, sound_count, window = feet_ref.shape
    rows = mine_ref.shape[0]
    own = (mine_ref[:, :window] + theirs_ref[:, window:]).astype(jnp.bfloat16)
    other = (mine_ref[:, window:] + theirs_ref[:, :window]).astype(jnp.bfloat16)
    block_index = block_of_row((rows, sound_count), block_count)
    image = jnp.zeros((rows, sound_count), jnp.float32)
    for block in range(block_count):
        part = dot(own, feet_ref[block], ((1,), (1,)))
        part = part + dot(other, other_feet_ref[block], ((1,), (1,)))
        image = jnp.where(block_index == block, part, image)
    return image


def turn_kernel(tiles_ref, mine_ref, theirs_ref, feet_ref, other_feet_ref, table_ref, out_ref, image_ref, placed):
    image = sound(mine_ref, theirs_ref, feet_ref, other_feet_ref)
    image_ref[...] = image
    send_adjoint(image.astype(jnp.bfloat16), tiles_ref, feet_ref, table_ref, out_ref, placed)


def last_kernel(probe_count, mine_ref, theirs_ref, feet_ref, other_feet_ref, probes_ref, first_ref, sums_ref, second_ref):
    second = sound(mine_ref, theirs_ref, feet_ref, other_feet_ref)
    second_ref[...] = second
    probes = probes_ref[...]
    first = first_ref[...]
    block_count = second.shape[0] // probe_count
    lane = lax.broadcasted_iota(jnp.int32, (1, LANES), 1)
    row = jnp.zeros((1, LANES), jnp.float32)
    pairs = (
        (probes, probes),
        (probes, first),
        (first, first),
        (probes, second),
        (first, second),
        (second, second),
    )
    for place, (left, right) in enumerate(pairs):
        product = left * right
        for probe in range(probe_count):
            value = jnp.sum(
                product[probe * block_count : (probe + 1) * block_count], axis=0, keepdims=True
            )
            value = jnp.sum(value, axis=1, keepdims=True)
            row = jnp.where(lane == place * probe_count + probe, value, row)
    sums_ref[...] = jnp.broadcast_to(row, sums_ref.shape)


def finish_kernel(total_rows, half_ref, sums_ref, probes_ref, first_ref, second_ref, coefficients_ref, residual_ref):
    block_count, probe_count, half_sound = residual_ref.shape
    row = jnp.sum(sums_ref[...], axis=0, keepdims=True) / total_rows

    def stat(place):
        shift = (LANES - place * probe_count) % LANES
        return row if shift == 0 else pltpu.roll(row, shift, 1)

    pp, pw, ww, px, wx, xx = [stat(place) for place in range(6)]
    scale_square = pp + epsilon
    scale = jnp.sqrt(scale_square)
    alpha_one = pw / scale_square
    rest = (ww - 2.0 * alpha_one * pw + alpha_one * alpha_one * pp) / scale_square
    beta_one = jnp.sqrt(jnp.maximum(rest, 0.0) + epsilon)
    cross = wx - alpha_one * ww - alpha_one * px + alpha_one * alpha_one * pw
    alpha_two = (cross / (beta_one * beta_one) - (pw - alpha_one * pp)) / scale_square
    of_second = 1.0 / (scale * beta_one)
    of_first = -(alpha_one + alpha_two) * of_second
    of_probes = (alpha_one * alpha_two / beta_one - beta_one) / scale
    square = (
        of_second * of_second * xx
        + of_first * of_first * ww
        + of_probes * of_probes * pp
        + 2.0 * (of_second * of_first * wx + of_second * of_probes * px + of_first * of_probes * pw)
    )
    beta_two = jnp.sqrt(jnp.maximum(square, 0.0) + epsilon)
    for place, value in enumerate((alpha_one, beta_one, alpha_two, beta_two)):
        coefficients_ref[place : place + 1, :] = value[:, :probe_count]
    at = pl.multiple_of(half_ref[0] * half_sound, LANES)
    for probe in range(probe_count):
        rows = slice(probe * block_count, (probe + 1) * block_count)
        residual_ref[:, probe, :] = (
            of_second[:, probe : probe + 1] * second_ref[rows, pl.ds(at, half_sound)]
            + of_first[:, probe : probe + 1] * first_ref[rows, pl.ds(at, half_sound)]
            + of_probes[:, probe : probe + 1] * probes_ref[rows, pl.ds(at, half_sound)]
        )


def make_table(owners, lag_weights):
    block_count, top_count = owners.shape
    parts = [owners.astype(jnp.float32)]
    rest = lag_weights
    for _ in range(3):
        part = lax.reduce_precision(rest, 8, 7)
        parts.append(part)
        rest = rest - part
    table = jnp.concatenate(parts, axis=1)
    return jnp.pad(table, ((0, 0), (HALF_LANES, LANES - HALF_LANES - 4 * top_count)))


def distance_terms(cells, sign):
    x, y = cells[0], cells[1]
    norm = x * x + y * y
    low = norm & 255
    one = jnp.ones_like(x)
    if sign > 0:
        terms = [x, y, norm - low, low, one, one]
    else:
        terms = [-2 * x, -2 * y, one, one, norm - low, low]
    terms = jnp.stack(terms).astype(jnp.bfloat16)
    return jnp.pad(terms, ((0, 16 - terms.shape[0]), (0, 0)))


def body(probes, footprints, lag_weights, owners, window_tiles, coords, temporal):
    periods = lax.axis_size("period")
    half_index = lax.axis_index("half")
    block_count, top_count = owners.shape
    probe_count = probes.shape[1]
    sound_count = footprints.shape[1]
    window = footprints.shape[2]
    cell_count = coords.shape[1]
    half_cells = cell_count // 2
    rows = block_count * probe_count
    total_rows = float(block_count * periods * sound_count)
    f32, bf16 = jnp.float32, jnp.bfloat16
    shape = jax.ShapeDtypeStruct
    wire = shape((periods * block_count, LANES), bf16)

    other_probes = from_other_half(probes)
    other_tiles = from_other_half(window_tiles)
    other_feet = from_other_half(footprints)
    half = half_index.astype(jnp.int32).reshape(1)
    table = make_table(owners, lag_weights)

    own_cells = lax.dynamic_slice_in_dim(coords, half_index * half_cells, half_cells, 1)
    other_cells = lax.dynamic_slice_in_dim(coords, (1 - half_index) * half_cells, half_cells, 1)
    left = distance_terms(own_cells, 1)
    right = distance_terms(jnp.concatenate([own_cells, other_cells], axis=1), -1)
    depth = 256
    spatial = pl.pallas_call(
        spatial_build_kernel,
        out_shape=shape((half_cells, cell_count), bf16),
        grid=(half_cells // depth,),
        in_specs=[
            pl.BlockSpec((16, depth), lambda i: (0, i)),
            pl.BlockSpec((16, cell_count), lambda i: (0, 0)),
        ],
        out_specs=pl.BlockSpec((depth, cell_count), lambda i: (i, 0)),
        name="spatial_build",
    )(left, right)

    def send(value):
        return exchange(value.reshape(periods, block_count, LANES)).reshape(value.shape)

    def spatial_step(received):
        mine = pl.pallas_call(
            functools.partial(spatial_kernel, block_count),
            out_shape=shape((rows, 2 * window), f32),
            grid=(half_cells // depth,),
            in_specs=[
                smem,
                smem,
                pl.BlockSpec(received.shape, lambda i: (0, 0)),
                pl.BlockSpec((depth, cell_count), lambda i: (i, 0)),
            ],
            out_specs=pl.BlockSpec((rows, 2 * window), lambda i: (0, 0)),
            scratch_shapes=[
                pltpu.VMEM((rows, half_cells), f32),
                pltpu.VMEM((rows, cell_count), f32),
            ],
            name="spatial_step",
        )(window_tiles, other_tiles, received, spatial)
        return mine, from_other_half(mine)

    placed = [pltpu.VMEM((rows, half_cells), f32)]
    to_mix, all_probes = pl.pallas_call(
        start_kernel,
        out_shape=(wire, shape((rows, sound_count), f32)),
        in_specs=[smem, smem, vmem, vmem, vmem, vmem],
        out_specs=(vmem, vmem),
        scratch_shapes=placed,
        name="start",
    )(half, window_tiles, probes, other_probes, footprints, table)
    mixed, choice = pl.pallas_call(
        functools.partial(first_mix_kernel, top_count),
        out_shape=(wire, shape((periods * block_count, 2 * periods), bf16)),
        in_specs=[vmem, vmem],
        out_specs=(vmem, vmem),
        name="first_mix",
    )(send(to_mix), temporal)
    mine, theirs = spatial_step(send(mixed))
    to_mix, first = pl.pallas_call(
        turn_kernel,
        out_shape=(wire, shape((rows, sound_count), f32)),
        in_specs=[smem, vmem, vmem, vmem, vmem, vmem],
        out_specs=(vmem, vmem),
        scratch_shapes=placed,
        name="turn",
    )(window_tiles, mine, theirs, footprints, other_feet, table)
    mixed = pl.pallas_call(
        mix_kernel, out_shape=wire, in_specs=[vmem, vmem, vmem], out_specs=vmem, name="second_mix"
    )(send(to_mix), temporal, choice)
    mine, theirs = spatial_step(send(mixed))
    sums, second = pl.pallas_call(
        functools.partial(last_kernel, probe_count),
        out_shape=(shape((periods, LANES), f32), shape((rows, sound_count), f32)),
        in_specs=[vmem] * 6,
        out_specs=(vmem, vmem),
        name="last",
    )(mine, theirs, footprints, other_feet, all_probes, first)
    sums = exchange(sums.reshape(periods, 1, LANES)).reshape(periods, LANES)
    return pl.pallas_call(
        functools.partial(finish_kernel, total_rows),
        out_shape=(shape((4, probe_count), f32), shape(probes.shape, f32)),
        in_specs=[smem, vmem, vmem, vmem, vmem],
        out_specs=(vmem, vmem),
        name="finish",
    )(half, sums, all_probes, first, second)


def solution(mesh):
    in_specs = (
        P("period", None, "half"),
        P("period", None, "half"),
        P("period", None),
        P("period", None),
        P("period", "half"),
        P(),
        P(),
    )
    out_specs = (P(), P("period", None, "half"))
    return jax.shard_map(body, mesh=mesh, in_specs=in_specs, out_specs=out_specs, check_vma=False)
```

```python
import functools

import jax
import jax.numpy as jnp
from jax import lax
from jax.experimental import pallas as pl
from jax.experimental.pallas import tpu as pltpu
from jax.sharding import PartitionSpec as P

epsilon = 1e-06
kernel_scale = 0.05
kernel_length = 6.0
log2e = 1.4426950408889634
LANES = 128
HALF_LANES = 64
HALF_SUBLANES = 4


smem = pl.BlockSpec(memory_space=pltpu.SMEM)
vmem = pl.BlockSpec(memory_space=pltpu.VMEM)
hbm = pl.BlockSpec(memory_space=pltpu.HBM)
small = pltpu.CompilerParams(vmem_limit_bytes=24 * 1024 * 1024)


def in_hbm(value):
    return pltpu.with_memory_space_constraint(value, pltpu.HBM)


def in_vmem(value):
    return pltpu.with_memory_space_constraint(value, pltpu.VMEM)


def from_other_half(value):
    return lax.ppermute(value, "half", [(0, 1), (1, 0)])


def exchange(value):
    return lax.all_to_all(value, "period", split_axis=0, concat_axis=0, tiled=True)


def block_of_row(shape, block_count):
    return lax.rem(lax.broadcasted_iota(jnp.int32, shape, 0), block_count)


def halves(value):
    high = value.astype(jnp.bfloat16)
    low = (value - high.astype(jnp.float32)).astype(jnp.bfloat16)
    return high, low


def dot(left, right, dims=((1,), (0,))):
    return lax.dot_general(left, right, (dims, ((), ())), preferred_element_type=jnp.float32)


def tile_iotas():
    row = lax.broadcasted_iota(jnp.int32, (2 * HALF_SUBLANES, LANES), 0)
    lane = lax.broadcasted_iota(jnp.int32, (2 * HALF_SUBLANES, LANES), 1)
    return row, lane


def half_turn(tile):
    return pltpu.roll(tile, HALF_SUBLANES, 0)


def swap_quarters(tile):
    row, lane = tile_iotas()
    turned = half_turn(pltpu.roll(tile, HALF_LANES, 1))
    return jnp.where((row < HALF_SUBLANES) == (lane < HALF_LANES), tile, turned)


def place_adjoint(vector, tiles_ref, feet_ref, placed, copies=()):
    block_count, _, window = feet_ref.shape
    piece_block = block_of_row((vector.shape[0], window), block_count)
    placed[...] = jnp.zeros_like(placed)
    for block in range(block_count):
        if copies:
            copies[block].wait()
        piece = dot(vector, feet_ref[block])
        start = pl.multiple_of(tiles_ref[block] * LANES, LANES)
        old = placed[:, pl.ds(start, window)]
        placed[:, pl.ds(start, window)] = jnp.where(piece_block == block, piece, old)


def placed_tile(placed, place, probe_count):
    tile, probe = divmod(place, probe_count)
    count = placed.shape[0] // probe_count
    return placed[probe * count : (probe + 1) * count, tile * LANES : (tile + 1) * LANES]


def prepare_kernel(owners_in, weights_in, own_in, own_ref, table_ref, owners_ref, weights_ref, probes_ref, sems):
    block_count, probe_count, _ = probes_ref.shape
    top_count = owners_ref.shape[0]
    pairs = ((owners_in, owners_ref), (weights_in, weights_ref), (own_in, probes_ref))
    copies = [
        pltpu.make_async_copy(source, target, sems.at[place])
        for place, (source, target) in enumerate(pairs)
    ]
    for copy in copies:
        copy.start()
    for copy in copies:
        copy.wait()
    for probe in range(probe_count):
        rows = slice(probe * block_count, (probe + 1) * block_count)
        own_ref[rows, :] = probes_ref[:, probe, :]
    row, lane = tile_iotas()
    owner = jnp.zeros(row.shape, jnp.float32)
    weight = jnp.zeros(row.shape, jnp.float32)
    for block in range(block_count):
        column, turn = divmod(block, HALF_SUBLANES)
        for top in range(top_count):
            here = (row == HALF_SUBLANES + turn) & (lane == column * HALF_LANES + top)
            owner = jnp.where(here, owners_ref[top, block].astype(jnp.float32), owner)
            weight = jnp.where(here, weights_ref[top, block], weight)
    table = owner
    for part in range(1, 4):
        high = weight.astype(jnp.bfloat16).astype(jnp.float32)
        table = table + pltpu.roll(high, part * top_count, 1)
        weight = weight - high
    table_ref[...] = table


def start_kernel(half_ref, own_ref, other_ref, table_ref, tiles_in, feet_in, out_ref, probes_ref, placed, tiles_ref, feet_ref, sems):
    tiles_copy = pltpu.make_async_copy(tiles_in, tiles_ref, sems.at[feet_ref.shape[0]])
    tiles_copy.start()
    feet_copies = [
        pltpu.make_async_copy(feet_in.at[block], feet_ref.at[block], sems.at[block])
        for block in range(feet_ref.shape[0])
    ]
    for copy in feet_copies:
        copy.start()
    half = half_ref[0]
    block_count, probe_count, half_sound = other_ref.shape
    own_at = pl.multiple_of(half * half_sound, LANES)
    other_at = pl.multiple_of((1 - half) * half_sound, LANES)
    probes_ref[:, pl.ds(own_at, half_sound)] = own_ref[...]
    for probe in range(probe_count):
        rows = slice(probe * block_count, (probe + 1) * block_count)
        probes_ref[rows, pl.ds(other_at, half_sound)] = other_ref[:, probe, :]
    vector = probes_ref[...].astype(jnp.bfloat16)
    tiles_copy.wait()
    place_adjoint(vector, tiles_ref, feet_ref, placed, feet_copies)
    table = table_ref[...]
    row, _ = tile_iotas()
    upper = row < HALF_SUBLANES
    count = placed.shape[1] // LANES * probe_count
    for place in range(count):
        tile = swap_quarters(placed_tile(placed, place, probe_count))
        pair = [jnp.where(upper, tile, table), jnp.where(upper, half_turn(tile), table)]
        at = 2 * block_count * place
        out_ref[at : at + 2 * block_count, :] = jnp.concatenate(pair, axis=0).astype(jnp.bfloat16)
    used = 2 * block_count * count
    out_ref[used:, :] = jnp.zeros((out_ref.shape[0] - used, LANES), jnp.bfloat16)


def distance_terms(cells, turned):
    x, y = cells[0:1], cells[1:2]
    norm = x * x + y * y
    low = (norm & 255).astype(jnp.float32)
    high = (norm - (norm & 255)).astype(jnp.float32)
    x, y, one = x.astype(jnp.float32), y.astype(jnp.float32), jnp.ones(x.shape, jnp.float32)
    if turned:
        terms = [-2.0 * x, -2.0 * y, one, one, high, low]
    else:
        terms = [x, y, high, low, one, one]
    row = lax.broadcasted_iota(jnp.int32, (16, x.shape[1]), 0)
    result = jnp.zeros((16, x.shape[1]), jnp.float32)
    for place, term in enumerate(terms):
        result = jnp.where(row == place, term, result)
    return result.astype(jnp.bfloat16)


def spatial_build_kernel(turned, half_ref, coords_ref, out_ref, left, right):
    half_cells = left.shape[1]
    depth = out_ref.shape[0]
    step = pl.program_id(0)

    @pl.when(step == 0)
    def _():
        half = half_ref[0]
        own_at = pl.multiple_of(half * half_cells, LANES)
        left[...] = distance_terms(coords_ref[:, pl.ds(own_at, half_cells)], False)
        side = 1 - half if turned else half
        at = pl.multiple_of(side * half_cells, LANES)
        right[...] = distance_terms(coords_ref[:, pl.ds(at, half_cells)], True)

    at = pl.multiple_of(step * depth, depth)
    squared = dot(left[:, pl.ds(at, depth)], right[...], ((0,), (0,)))
    squared = jnp.maximum(squared, 1e-12)
    distance = squared * lax.rsqrt(squared)
    out_ref[...] = jnp.exp2(distance * (-log2e / kernel_length)).astype(jnp.bfloat16)


def mix(received, choice, temporal):
    periods = temporal.shape[0]
    lane = lax.broadcasted_iota(jnp.int32, (periods, LANES), 1)
    both = dot(choice, received, ((0,), (0,)))
    both = both[: 2 * periods] + both[2 * periods :]
    gathered = both[:periods] + pltpu.roll(both[periods:], HALF_LANES, 1)
    gathered = jnp.where(lane < HALF_LANES, gathered, 0.0)
    mixed = lax.dot_general(
        temporal,
        gathered * kernel_scale,
        (((1,), (0,)), ((), ())),
        precision=lax.Precision.HIGHEST,
        preferred_element_type=jnp.float32,
    )
    high, low = halves(jnp.concatenate([mixed, pltpu.roll(mixed, HALF_LANES, 1)], axis=0))
    upper, lower = choice[:, : 2 * periods], choice[:, 2 * periods :]
    return (dot(upper, high) + dot(lower, high) + dot(upper, low)).astype(jnp.bfloat16)


def first_mix_kernel(top_count, received_ref, temporal_ref, out_ref, choice_ref, data, tables):
    periods = temporal_ref.shape[0]
    row, _ = tile_iotas()
    upper = row < HALF_SUBLANES
    size = row.shape[0]
    for pair in range(data.shape[0] // size):
        both = received_ref[2 * size * pair : 2 * size * (pair + 1), :].astype(jnp.float32)
        one, two = both[:size], both[size:]
        at = slice(size * pair, size * (pair + 1))
        data[at, :] = jnp.where(upper, one, half_turn(two))
        tables[at, :] = jnp.where(upper, half_turn(one), two)
    wide = tables[...]
    lane = lax.broadcasted_iota(jnp.int32, (wide.shape[0], periods), 1).astype(jnp.float32)
    for column in range(2):
        choice = jnp.zeros((wide.shape[0], periods), jnp.float32)
        for top in range(top_count):
            at = column * HALF_LANES + top
            owner = wide[:, at : at + 1]
            weight = (
                wide[:, at + top_count : at + top_count + 1]
                + wide[:, at + 2 * top_count : at + 2 * top_count + 1]
                + wide[:, at + 3 * top_count : at + 3 * top_count + 1]
            )
            choice = choice + jnp.where(owner == lane, weight, 0.0)
        high, low = halves(choice)
        choice_ref[:, column * periods : (column + 1) * periods] = high
        choice_ref[:, (2 + column) * periods : (3 + column) * periods] = low
    out_ref[...] = mix(data[...].astype(jnp.bfloat16), choice_ref[...], temporal_ref[...])


def mix_kernel(received_ref, temporal_ref, choice_ref, out_ref):
    out_ref[...] = mix(received_ref[...], choice_ref[...], temporal_ref[...])


def spatial_kernel(block_count, streamed, tiles_ref, others_ref, received_ref, *refs):
    if streamed:
        own_spatial, other_spatial, out_ref, kept_ref, field, total, *stream = refs
    else:
        kept_ref, out_ref, field, total = refs
        own_spatial, other_spatial = None, None
    rows, half_cells = field.shape
    probe_count = rows // block_count
    width = 512
    chunks = [
        (side, slice(at, at + width))
        for side in (own_spatial, other_spatial)
        for at in range(0, half_cells, width)
    ]
    copies = []
    if streamed:
        buffers, sems = kept_ref, stream[0]
        copies = [
            pltpu.make_async_copy(side.at[:, at], buffers.at[place], sems.at[place])
            for place, (side, at) in enumerate(chunks)
        ]
        for copy in copies:
            copy.start()
    for pair in range(half_cells // LANES * probe_count // 2):
        both = received_ref[2 * block_count * pair : 2 * block_count * (pair + 1), :]
        both = both.astype(jnp.float32)
        for part in range(2):
            tile, probe = divmod(2 * pair + part, probe_count)
            value = swap_quarters(both[part * block_count : (part + 1) * block_count])
            field[
                probe * block_count : (probe + 1) * block_count, tile * LANES : (tile + 1) * LANES
            ] = value
    cells = field[...].astype(jnp.bfloat16)
    for place, (side, at) in enumerate(chunks):
        if streamed:
            copies[place].wait()
        total[:, place * width : (place + 1) * width] = dot(cells, kept_ref[place])
    window = out_ref.shape[1] // 2
    block_index = block_of_row((rows, window), block_count)
    own = jnp.zeros((rows, window), jnp.float32)
    other = jnp.zeros((rows, window), jnp.float32)
    for block in range(block_count):
        own_at = pl.multiple_of(tiles_ref[block] * LANES, LANES)
        other_at = pl.multiple_of(half_cells + others_ref[block] * LANES, LANES)
        own = jnp.where(block_index == block, total[:, pl.ds(own_at, window)], own)
        other = jnp.where(block_index == block, total[:, pl.ds(other_at, window)], other)
    out_ref[:, :window] = own
    out_ref[:, window:] = other


def sound(mine_ref, theirs_ref, feet_ref, other_feet_ref):
    block_count, sound_count, window = feet_ref.shape
    rows = mine_ref.shape[0]
    own = (mine_ref[:, :window] + theirs_ref[:, window:]).astype(jnp.bfloat16)
    other = (mine_ref[:, window:] + theirs_ref[:, :window]).astype(jnp.bfloat16)
    block_index = block_of_row((rows, sound_count), block_count)
    image = jnp.zeros((rows, sound_count), jnp.float32)
    for block in range(block_count):
        part = dot(own, feet_ref[block], ((1,), (1,)))
        part = part + dot(other, other_feet_ref[block], ((1,), (1,)))
        image = jnp.where(block_index == block, part, image)
    return image


def turn_kernel(tiles_ref, mine_ref, theirs_ref, feet_ref, other_feet_ref, out_ref, image_ref, placed):
    image = sound(mine_ref, theirs_ref, feet_ref, other_feet_ref)
    image_ref[...] = image
    place_adjoint(image.astype(jnp.bfloat16), tiles_ref, feet_ref, placed)
    block_count = feet_ref.shape[0]
    probe_count = image.shape[0] // block_count
    count = placed.shape[1] // LANES * probe_count
    for pair in range(count // 2):
        tiles = [
            swap_quarters(placed_tile(placed, 2 * pair + part, probe_count)) for part in range(2)
        ]
        at = 2 * block_count * pair
        out_ref[at : at + 2 * block_count, :] = jnp.concatenate(tiles, axis=0).astype(jnp.bfloat16)
    used = block_count * count
    out_ref[used:, :] = jnp.zeros((out_ref.shape[0] - used, LANES), jnp.bfloat16)


def last_kernel(probe_count, mine_ref, theirs_ref, feet_ref, other_feet_ref, probes_ref, first_ref, sums_ref, second_ref):
    second = sound(mine_ref, theirs_ref, feet_ref, other_feet_ref)
    second_ref[...] = second
    probes = probes_ref[...]
    first = first_ref[...]
    block_count = second.shape[0] // probe_count
    lane = lax.broadcasted_iota(jnp.int32, (1, LANES), 1)
    row = jnp.zeros((1, LANES), jnp.float32)
    pairs = (
        (probes, probes),
        (probes, first),
        (first, first),
        (probes, second),
        (first, second),
        (second, second),
    )
    for place, (left, right) in enumerate(pairs):
        product = left * right
        for probe in range(probe_count):
            value = jnp.sum(
                product[probe * block_count : (probe + 1) * block_count], axis=0, keepdims=True
            )
            value = jnp.sum(value, axis=1, keepdims=True)
            row = jnp.where(lane == place * probe_count + probe, value, row)
    sums_ref[...] = jnp.broadcast_to(row, sums_ref.shape)


def finish_kernel(total_rows, half_ref, sums_ref, probes_ref, first_ref, second_ref, coefficients_ref, residual_ref):
    block_count, probe_count, half_sound = residual_ref.shape
    row = jnp.sum(sums_ref[...], axis=0, keepdims=True) / total_rows

    def stat(place):
        shift = (LANES - place * probe_count) % LANES
        return row if shift == 0 else pltpu.roll(row, shift, 1)

    pp, pw, ww, px, wx, xx = [stat(place) for place in range(6)]
    scale_square = pp + epsilon
    scale = jnp.sqrt(scale_square)
    alpha_one = pw / scale_square
    rest = (ww - 2.0 * alpha_one * pw + alpha_one * alpha_one * pp) / scale_square
    beta_one = jnp.sqrt(jnp.maximum(rest, 0.0) + epsilon)
    cross = wx - alpha_one * ww - alpha_one * px + alpha_one * alpha_one * pw
    alpha_two = (cross / (beta_one * beta_one) - (pw - alpha_one * pp)) / scale_square
    of_second = 1.0 / (scale * beta_one)
    of_first = -(alpha_one + alpha_two) * of_second
    of_probes = (alpha_one * alpha_two / beta_one - beta_one) / scale
    square = (
        of_second * of_second * xx
        + of_first * of_first * ww
        + of_probes * of_probes * pp
        + 2.0 * (of_second * of_first * wx + of_second * of_probes * px + of_first * of_probes * pw)
    )
    beta_two = jnp.sqrt(jnp.maximum(square, 0.0) + epsilon)
    for place, value in enumerate((alpha_one, beta_one, alpha_two, beta_two)):
        coefficients_ref[place : place + 1, :] = value[:, :probe_count]
    at = pl.multiple_of(half_ref[0] * half_sound, LANES)
    for probe in range(probe_count):
        rows = slice(probe * block_count, (probe + 1) * block_count)
        residual_ref[:, probe, :] = (
            of_second[:, probe : probe + 1] * second_ref[rows, pl.ds(at, half_sound)]
            + of_first[:, probe : probe + 1] * first_ref[rows, pl.ds(at, half_sound)]
            + of_probes[:, probe : probe + 1] * probes_ref[rows, pl.ds(at, half_sound)]
        )


def body(probes, footprints, lag_weights, owners, window_tiles, coords, temporal):
    periods = lax.axis_size("period")
    half_index = lax.axis_index("half")
    block_count, top_count = owners.shape
    probe_count = probes.shape[1]
    sound_count = footprints.shape[1]
    window = footprints.shape[2]
    cell_count = coords.shape[1]
    half_cells = cell_count // 2
    rows = block_count * probe_count
    total_rows = float(block_count * periods * sound_count)
    f32, bf16 = jnp.float32, jnp.bfloat16
    wire = pltpu.VMEM((periods * HALF_SUBLANES, LANES), bf16)
    vectors = pltpu.VMEM((rows, sound_count), f32)
    placed = [pltpu.VMEM((rows, half_cells), f32)]

    def call(kernel, name, scalars, values, outputs, scratch=(), left_in_hbm=()):
        outputs = tuple(outputs)
        results = pl.pallas_call(
            kernel,
            out_shape=outputs,
            in_specs=[smem] * len(scalars) + [vmem] * len(values) + [hbm] * len(left_in_hbm),
            out_specs=tuple(vmem for _ in outputs),
            scratch_shapes=list(scratch),
            compiler_params=small,
            name=name,
        )(
            *scalars,
            *[in_vmem(value) for value in values],
            *[in_hbm(value) for value in left_in_hbm],
        )
        return results if len(outputs) > 1 else results[0]

    def send(value):
        count = value.shape[0] // periods
        return exchange(value.reshape(periods, count, LANES)).reshape(value.shape)

    def build_spatial(turned):
        depth = 256
        return pl.pallas_call(
            functools.partial(spatial_build_kernel, turned),
            out_shape=pltpu.HBM((half_cells, half_cells), bf16),
            grid=(half_cells // depth,),
            in_specs=[smem, pl.BlockSpec((2, cell_count), lambda i: (0, 0))],
            out_specs=pl.BlockSpec((depth, half_cells), lambda i: (i, 0)),
            scratch_shapes=[pltpu.VMEM((16, half_cells), bf16)] * 2,
            compiler_params=small,
            name="spatial_build",
        )(half, coords)

    def spatial_step(received, kept):
        scratch = [pltpu.VMEM((rows, half_cells), f32), pltpu.VMEM((rows, cell_count), f32)]
        outputs = [pltpu.VMEM((rows, 2 * window), f32)]
        values, stored = (received,), ()
        if kept is None:
            count = cell_count // 512
            outputs.append(pltpu.VMEM((count, half_cells, 512), bf16))
            scratch.append(pltpu.SemaphoreType.DMA((count,)))
            stored = (own_spatial, other_spatial)
        else:
            values = (received, kept)
        results = call(
            functools.partial(spatial_kernel, block_count, kept is None),
            "spatial_step",
            (tiles, other_tiles),
            values,
            outputs,
            scratch,
            stored,
        )
        mine, kept = results if kept is None else (results, kept)
        return mine, from_other_half(mine), kept

    half = half_index.astype(jnp.int32).reshape(1)
    tiles = window_tiles.reshape(-1)
    other_probes = from_other_half(probes)
    own_probes, table = call(
        prepare_kernel,
        "prepare",
        (),
        (),
        (pltpu.VMEM((rows, sound_count // 2), f32), pltpu.VMEM((2 * HALF_SUBLANES, LANES), f32)),
        (
            pltpu.SMEM((top_count, block_count), jnp.int32),
            pltpu.SMEM((top_count, block_count), f32),
            pltpu.VMEM(probes.shape, f32),
            pltpu.SemaphoreType.DMA((3,)),
        ),
        (owners.T, lag_weights.T, probes),
    )
    to_mix, all_probes = call(
        start_kernel,
        "start",
        (half,),
        (own_probes, other_probes, table),
        (pltpu.VMEM((periods * 2 * HALF_SUBLANES, LANES), bf16), vectors),
        placed
        + [
            pltpu.SMEM(tiles.shape, jnp.int32),
            pltpu.VMEM(footprints.shape, bf16),
            pltpu.SemaphoreType.DMA((block_count + 1,)),
        ],
        (tiles, footprints),
    )
    later_feet, later_tiles, to_mix = lax.optimization_barrier((footprints, tiles, to_mix))
    other_feet = from_other_half(later_feet)
    other_tiles = from_other_half(later_tiles)
    own_spatial = build_spatial(False)
    received, own_spatial, other_tiles = lax.optimization_barrier(
        (send(to_mix), own_spatial, other_tiles)
    )
    mixed, choice = call(
        functools.partial(first_mix_kernel, top_count),
        "first_mix",
        (),
        (received, temporal),
        (wire, pltpu.VMEM((periods * HALF_SUBLANES, 4 * periods), bf16)),
        [pltpu.VMEM((periods * HALF_SUBLANES, LANES), f32)] * 2,
    )
    other_spatial = build_spatial(True)
    mine, theirs, kept = spatial_step(send(mixed), None)
    to_mix, first = call(
        turn_kernel,
        "turn",
        (tiles,),
        (mine, theirs, footprints, other_feet),
        (wire, vectors),
        placed,
    )
    mixed = call(mix_kernel, "second_mix", (), (send(to_mix), temporal, choice), (wire,))
    mine, theirs, kept = spatial_step(send(mixed), kept)
    sums, second = call(
        functools.partial(last_kernel, probe_count),
        "last",
        (),
        (mine, theirs, footprints, other_feet, all_probes, first),
        (pltpu.VMEM((periods, LANES), f32), vectors),
    )
    sums = exchange(sums.reshape(periods, 1, LANES)).reshape(periods, LANES)
    return pl.pallas_call(
        functools.partial(finish_kernel, total_rows),
        out_shape=(
            jax.ShapeDtypeStruct((4, probe_count), f32),
            jax.ShapeDtypeStruct(probes.shape, f32),
        ),
        in_specs=[smem, vmem, vmem, vmem, vmem],
        out_specs=(vmem, vmem),
        compiler_params=small,
        name="finish",
    )(half, in_vmem(sums), in_vmem(all_probes), in_vmem(first), in_vmem(second))


def solution(mesh):
    in_specs = (
        P("period", None, "half"),
        P("period", None, "half"),
        P("period", None),
        P("period", None),
        P("period", "half"),
        P(),
        P(),
    )
    out_specs = (P(), P("period", None, "half"))
    return jax.shard_map(body, mesh=mesh, in_specs=in_specs, out_specs=out_specs, check_vma=False)
```

```python
import functools

import jax
import jax.numpy as jnp
from jax import lax
from jax.experimental import pallas as pl
from jax.experimental.pallas import tpu as pltpu
from jax.sharding import PartitionSpec as P

epsilon = 1e-06
kernel_scale = 0.05
kernel_length = 6.0
log2e = 1.4426950408889634
LANES = 128
HALF_LANES = 64
HALF_SUBLANES = 4


smem = pl.BlockSpec(memory_space=pltpu.SMEM)
vmem = pl.BlockSpec(memory_space=pltpu.VMEM)
hbm = pl.BlockSpec(memory_space=pltpu.HBM)
small = pltpu.CompilerParams(vmem_limit_bytes=24 * 1024 * 1024)


def in_hbm(value):
    return pltpu.with_memory_space_constraint(value, pltpu.HBM)


def in_vmem(value):
    return pltpu.with_memory_space_constraint(value, pltpu.VMEM)


def from_other_half(value):
    return lax.ppermute(value, "half", [(0, 1), (1, 0)])


def exchange(value):
    return lax.all_to_all(value, "period", split_axis=0, concat_axis=0, tiled=True)


def block_of_row(shape, block_count):
    return lax.rem(lax.broadcasted_iota(jnp.int32, shape, 0), block_count)


def halves(value):
    high = value.astype(jnp.bfloat16)
    low = (value - high.astype(jnp.float32)).astype(jnp.bfloat16)
    return high, low


def dot(left, right, dims=((1,), (0,))):
    return lax.dot_general(left, right, (dims, ((), ())), preferred_element_type=jnp.float32)


def tile_iotas():
    row = lax.broadcasted_iota(jnp.int32, (2 * HALF_SUBLANES, LANES), 0)
    lane = lax.broadcasted_iota(jnp.int32, (2 * HALF_SUBLANES, LANES), 1)
    return row, lane


def half_turn(tile):
    return pltpu.roll(tile, HALF_SUBLANES, 0)


def swap_quarters(tile):
    row, lane = tile_iotas()
    turned = half_turn(pltpu.roll(tile, HALF_LANES, 1))
    return jnp.where((row < HALF_SUBLANES) == (lane < HALF_LANES), tile, turned)


def adjoint_pieces(vector, feet_ref):
    block_count, _, window = feet_ref.shape
    block_index = block_of_row((vector.shape[0], window), block_count)
    pieces = jnp.zeros((vector.shape[0], window), jnp.float32)
    for block in range(block_count):
        pieces = jnp.where(block_index == block, dot(vector, feet_ref[block]), pieces)
    return pieces


def placed_tile(pieces, tile_rows, place, probe_count):
    tile, probe = divmod(place, probe_count)
    count = pieces.shape[0] // probe_count
    rows = slice(probe * count, (probe + 1) * count)
    value = jnp.where(tile_rows == tile, pieces[rows, :LANES], 0.0)
    return swap_quarters(jnp.where(tile_rows == tile - 1, pieces[rows, LANES:], value))


def prepare_kernel(tiles_in, owners_in, weights_in, own_in, feet_in, own_ref, table_ref, tile_rows_ref, feet_ref, tiles_ref, owners_ref, weights_ref, probes_ref, sems):
    block_count, probe_count, _ = probes_ref.shape
    top_count = owners_ref.shape[0]
    pairs = (
        (tiles_in, tiles_ref),
        (owners_in, owners_ref),
        (weights_in, weights_ref),
        (own_in, probes_ref),
        (feet_in, feet_ref),
    )
    copies = [
        pltpu.make_async_copy(source, target, sems.at[place])
        for place, (source, target) in enumerate(pairs)
    ]
    for copy in copies:
        copy.start()
    for copy in copies[:4]:
        copy.wait()
    for probe in range(probe_count):
        rows = slice(probe * block_count, (probe + 1) * block_count)
        own_ref[rows, :] = probes_ref[:, probe, :]
    row, lane = tile_iotas()
    owner = jnp.zeros(row.shape, jnp.float32)
    weight = jnp.zeros(row.shape, jnp.float32)
    for block in range(block_count):
        column, turn = divmod(block, HALF_SUBLANES)
        for top in range(top_count):
            here = (row == HALF_SUBLANES + turn) & (lane == column * HALF_LANES + top)
            owner = jnp.where(here, owners_ref[top, block].astype(jnp.float32), owner)
            weight = jnp.where(here, weights_ref[top, block], weight)
    table = owner
    for part in range(1, 4):
        high = weight.astype(jnp.bfloat16).astype(jnp.float32)
        table = table + pltpu.roll(high, part * top_count, 1)
        weight = weight - high
    table_ref[...] = table
    tile_rows = jnp.zeros(row.shape, jnp.int32)
    for block in range(block_count):
        tile_rows = jnp.where(row == block, tiles_ref[block], tile_rows)
    tile_rows_ref[...] = tile_rows
    copies[4].wait()


def start_kernel(half_ref, own_ref, other_ref, table_ref, tile_rows_ref, feet_ref, others_ref, out_ref, probes_ref):
    half = half_ref[0]
    block_count, probe_count, half_sound = other_ref.shape
    own_at = pl.multiple_of(half * half_sound, LANES)
    other_at = pl.multiple_of((1 - half) * half_sound, LANES)
    probes_ref[:, pl.ds(own_at, half_sound)] = own_ref[...]
    for probe in range(probe_count):
        rows = slice(probe * block_count, (probe + 1) * block_count)
        probes_ref[rows, pl.ds(other_at, half_sound)] = other_ref[:, probe, :]
    pieces = adjoint_pieces(probes_ref[...].astype(jnp.bfloat16), feet_ref)
    table, tile_rows = table_ref[...], tile_rows_ref[...]
    row, _ = tile_iotas()
    upper = row < HALF_SUBLANES
    size = 2 * block_count
    count = out_ref.shape[0] // size * 3 // 4
    for place in range(count):
        tile = placed_tile(pieces, tile_rows, place, probe_count)
        pair = [jnp.where(upper, tile, table), jnp.where(upper, half_turn(tile), table)]
        out_ref[size * place : size * (place + 1), :] = jnp.concatenate(pair, axis=0).astype(
            jnp.bfloat16
        )
    out_ref[size * count :, :] = jnp.zeros((out_ref.shape[0] - size * count, LANES), jnp.bfloat16)


def distance_terms(cells, turned):
    x, y = cells[0:1], cells[1:2]
    norm = x * x + y * y
    low = (norm & 255).astype(jnp.float32)
    high = (norm - (norm & 255)).astype(jnp.float32)
    x, y, one = x.astype(jnp.float32), y.astype(jnp.float32), jnp.ones(x.shape, jnp.float32)
    if turned:
        terms = [-2.0 * x, -2.0 * y, one, one, high, low]
    else:
        terms = [x, y, high, low, one, one]
    row = lax.broadcasted_iota(jnp.int32, (16, x.shape[1]), 0)
    result = jnp.zeros((16, x.shape[1]), jnp.float32)
    for place, term in enumerate(terms):
        result = jnp.where(row == place, term, result)
    return result.astype(jnp.bfloat16)


def spatial_build_kernel(turned, half_ref, coords_ref, out_ref, left, right):
    half_cells = left.shape[1]
    depth = out_ref.shape[0]
    step = pl.program_id(0)

    @pl.when(step == 0)
    def _():
        half = half_ref[0]
        own_at = pl.multiple_of(half * half_cells, LANES)
        left[...] = distance_terms(coords_ref[:, pl.ds(own_at, half_cells)], False)
        side = 1 - half if turned else half
        at = pl.multiple_of(side * half_cells, LANES)
        right[...] = distance_terms(coords_ref[:, pl.ds(at, half_cells)], True)

    at = pl.multiple_of(step * depth, depth)
    squared = dot(left[:, pl.ds(at, depth)], right[...], ((0,), (0,)))
    squared = jnp.maximum(squared, 1e-12)
    distance = squared * lax.rsqrt(squared)
    out_ref[...] = jnp.exp2(distance * (-log2e / kernel_length)).astype(jnp.bfloat16)


def mix(received, choice, temporal):
    periods = temporal.shape[0]
    both = dot(choice, received)
    both = both[: 2 * periods] + both[2 * periods :]
    gathered = both[:periods] + pltpu.roll(both[periods:], HALF_LANES, 1)
    mixed = lax.dot_general(
        gathered * kernel_scale,
        temporal,
        (((0,), (1,)), ((), ())),
        precision=lax.Precision.HIGHEST,
        preferred_element_type=jnp.float32,
    )
    high, low = halves(mixed[:HALF_LANES])

    def columns(part):
        nothing = jnp.zeros(part.shape, part.dtype)
        upper = jnp.concatenate([part, nothing], axis=1)
        return jnp.concatenate([upper, jnp.concatenate([nothing, part], axis=1)], axis=0)

    high, low = columns(high), columns(low)
    upper, lower = choice[: 2 * periods], choice[2 * periods :]
    return (dot(high, upper) + dot(high, lower) + dot(low, upper)).T.astype(jnp.bfloat16)


def first_mix_kernel(top_count, received_ref, temporal_ref, out_ref, choice_ref, data, tables):
    periods = temporal_ref.shape[0]
    row, _ = tile_iotas()
    upper = row < HALF_SUBLANES
    size = row.shape[0]
    for pair in range(data.shape[0] // size):
        both = received_ref[2 * size * pair : 2 * size * (pair + 1), :].astype(jnp.float32)
        one, two = both[:size], both[size:]
        at = slice(size * pair, size * (pair + 1))
        data[at, :] = jnp.where(upper, one, half_turn(two))
        tables[at, :] = jnp.where(upper, half_turn(one), two)
    wide = tables[...].T
    shape = (periods, wide.shape[1])
    period = lax.broadcasted_iota(jnp.int32, shape, 0).astype(jnp.float32)
    for column in range(2):
        choice = jnp.zeros(shape, jnp.float32)
        for top in range(top_count):
            at = column * HALF_LANES + top
            owner = wide[at : at + 1]
            weight = (
                wide[at + top_count : at + top_count + 1]
                + wide[at + 2 * top_count : at + 2 * top_count + 1]
                + wide[at + 3 * top_count : at + 3 * top_count + 1]
            )
            choice = choice + jnp.where(owner == period, weight, 0.0)
        high, low = halves(choice)
        choice_ref[column * periods : (column + 1) * periods, :] = high
        choice_ref[(2 + column) * periods : (3 + column) * periods, :] = low
    out_ref[...] = mix(data[...].astype(jnp.bfloat16), choice_ref[...], temporal_ref[...])


def mix_kernel(received_ref, temporal_ref, choice_ref, out_ref):
    out_ref[...] = mix(received_ref[...], choice_ref[...], temporal_ref[...])


def spatial_kernel(block_count, streamed, tiles_ref, others_ref, received_ref, *refs):
    if streamed:
        own_spatial, other_spatial, out_ref, kept_ref, field, total, *stream = refs
    else:
        kept_ref, out_ref, field, total = refs
        own_spatial, other_spatial = None, None
    rows, half_cells = field.shape
    probe_count = rows // block_count
    width = 512
    chunks = [
        (side, slice(at, at + width))
        for side in (own_spatial, other_spatial)
        for at in range(0, half_cells, width)
    ]
    copies = []
    if streamed:
        buffers, sems = kept_ref, stream[0]
        copies = [
            pltpu.make_async_copy(side.at[:, at], buffers.at[place], sems.at[place])
            for place, (side, at) in enumerate(chunks)
        ]
        for copy in copies:
            copy.start()
    for pair in range(half_cells // LANES * probe_count // 2):
        both = received_ref[2 * block_count * pair : 2 * block_count * (pair + 1), :]
        both = both.astype(jnp.float32)
        for part in range(2):
            tile, probe = divmod(2 * pair + part, probe_count)
            value = swap_quarters(both[part * block_count : (part + 1) * block_count])
            field[
                probe * block_count : (probe + 1) * block_count, tile * LANES : (tile + 1) * LANES
            ] = value
    cells = field[...].astype(jnp.bfloat16)
    for place, (side, at) in enumerate(chunks):
        if streamed:
            copies[place].wait()
        total[:, place * width : (place + 1) * width] = dot(cells, kept_ref[place])
    window = out_ref.shape[1] // 2
    block_index = block_of_row((rows, window), block_count)
    own = jnp.zeros((rows, window), jnp.float32)
    other = jnp.zeros((rows, window), jnp.float32)
    for block in range(block_count):
        own_at = pl.multiple_of(tiles_ref[block] * LANES, LANES)
        other_at = pl.multiple_of(half_cells + others_ref[block] * LANES, LANES)
        own = jnp.where(block_index == block, total[:, pl.ds(own_at, window)], own)
        other = jnp.where(block_index == block, total[:, pl.ds(other_at, window)], other)
    out_ref[:, :window] = own
    out_ref[:, window:] = other


def sound(mine_ref, theirs_ref, feet_ref, other_feet_ref):
    block_count, sound_count, window = feet_ref.shape
    rows = mine_ref.shape[0]
    own = (mine_ref[:, :window] + theirs_ref[:, window:]).astype(jnp.bfloat16)
    other = (mine_ref[:, window:] + theirs_ref[:, :window]).astype(jnp.bfloat16)
    block_index = block_of_row((rows, sound_count), block_count)
    image = jnp.zeros((rows, sound_count), jnp.float32)
    for block in range(block_count):
        part = dot(own, feet_ref[block], ((1,), (1,)))
        part = part + dot(other, other_feet_ref[block], ((1,), (1,)))
        image = jnp.where(block_index == block, part, image)
    return image


def turn_kernel(mine_ref, theirs_ref, feet_ref, other_feet_ref, tile_rows_ref, out_ref, image_ref):
    image = sound(mine_ref, theirs_ref, feet_ref, other_feet_ref)
    image_ref[...] = image
    pieces = adjoint_pieces(image.astype(jnp.bfloat16), feet_ref)
    tile_rows = tile_rows_ref[...]
    size = 2 * feet_ref.shape[0]
    probe_count = image.shape[0] // feet_ref.shape[0]
    count = out_ref.shape[0] // size * 3 // 4
    for pair in range(count):
        tiles = [
            placed_tile(pieces, tile_rows, 2 * pair + part, probe_count) for part in range(2)
        ]
        out_ref[size * pair : size * (pair + 1), :] = jnp.concatenate(tiles, axis=0).astype(
            jnp.bfloat16
        )
    out_ref[size * count :, :] = jnp.zeros((out_ref.shape[0] - size * count, LANES), jnp.bfloat16)


def last_kernel(probe_count, mine_ref, theirs_ref, feet_ref, other_feet_ref, probes_ref, first_ref, sums_ref, second_ref):
    second = sound(mine_ref, theirs_ref, feet_ref, other_feet_ref)
    second_ref[...] = second
    probes = probes_ref[...]
    first = first_ref[...]
    block_count = second.shape[0] // probe_count
    lane = lax.broadcasted_iota(jnp.int32, (1, LANES), 1)
    row = jnp.zeros((1, LANES), jnp.float32)
    pairs = (
        (probes, probes),
        (probes, first),
        (first, first),
        (probes, second),
        (first, second),
        (second, second),
    )
    for place, (left, right) in enumerate(pairs):
        product = left * right
        for probe in range(probe_count):
            value = jnp.sum(
                product[probe * block_count : (probe + 1) * block_count], axis=0, keepdims=True
            )
            value = jnp.sum(value, axis=1, keepdims=True)
            row = jnp.where(lane == place * probe_count + probe, value, row)
    sums_ref[...] = jnp.broadcast_to(row, sums_ref.shape)


def finish_kernel(total_rows, half_ref, sums_ref, probes_ref, first_ref, second_ref, coefficients_ref, residual_ref):
    block_count, probe_count, half_sound = residual_ref.shape
    row = jnp.sum(sums_ref[...], axis=0, keepdims=True) / total_rows

    def stat(place):
        shift = (LANES - place * probe_count) % LANES
        return row if shift == 0 else pltpu.roll(row, shift, 1)

    pp, pw, ww, px, wx, xx = [stat(place) for place in range(6)]
    scale_square = pp + epsilon
    scale = jnp.sqrt(scale_square)
    alpha_one = pw / scale_square
    rest = (ww - 2.0 * alpha_one * pw + alpha_one * alpha_one * pp) / scale_square
    beta_one = jnp.sqrt(jnp.maximum(rest, 0.0) + epsilon)
    cross = wx - alpha_one * ww - alpha_one * px + alpha_one * alpha_one * pw
    alpha_two = (cross / (beta_one * beta_one) - (pw - alpha_one * pp)) / scale_square
    of_second = 1.0 / (scale * beta_one)
    of_first = -(alpha_one + alpha_two) * of_second
    of_probes = (alpha_one * alpha_two / beta_one - beta_one) / scale
    square = (
        of_second * of_second * xx
        + of_first * of_first * ww
        + of_probes * of_probes * pp
        + 2.0 * (of_second * of_first * wx + of_second * of_probes * px + of_first * of_probes * pw)
    )
    beta_two = jnp.sqrt(jnp.maximum(square, 0.0) + epsilon)
    for place, value in enumerate((alpha_one, beta_one, alpha_two, beta_two)):
        coefficients_ref[place : place + 1, :] = value[:, :probe_count]
    at = pl.multiple_of(half_ref[0] * half_sound, LANES)
    for probe in range(probe_count):
        rows = slice(probe * block_count, (probe + 1) * block_count)
        residual_ref[:, probe, :] = (
            of_second[:, probe : probe + 1] * second_ref[rows, pl.ds(at, half_sound)]
            + of_first[:, probe : probe + 1] * first_ref[rows, pl.ds(at, half_sound)]
            + of_probes[:, probe : probe + 1] * probes_ref[rows, pl.ds(at, half_sound)]
        )


def body(probes, footprints, lag_weights, owners, window_tiles, coords, temporal):
    periods = lax.axis_size("period")
    half_index = lax.axis_index("half")
    block_count, top_count = owners.shape
    probe_count = probes.shape[1]
    sound_count = footprints.shape[1]
    window = footprints.shape[2]
    cell_count = coords.shape[1]
    half_cells = cell_count // 2
    rows = block_count * probe_count
    total_rows = float(block_count * periods * sound_count)
    f32, bf16 = jnp.float32, jnp.bfloat16
    wire = pltpu.VMEM((periods * HALF_SUBLANES, LANES), bf16)
    vectors = pltpu.VMEM((rows, sound_count), f32)

    def call(kernel, name, scalars, values, outputs, scratch=(), left_in_hbm=()):
        outputs = tuple(outputs)
        results = pl.pallas_call(
            kernel,
            out_shape=outputs,
            in_specs=[smem] * len(scalars) + [vmem] * len(values) + [hbm] * len(left_in_hbm),
            out_specs=tuple(vmem for _ in outputs),
            scratch_shapes=list(scratch),
            compiler_params=small,
            name=name,
        )(
            *scalars,
            *[in_vmem(value) for value in values],
            *[in_hbm(value) for value in left_in_hbm],
        )
        return results if len(outputs) > 1 else results[0]

    def send(value):
        count = value.shape[0] // periods
        return exchange(value.reshape(periods, count, LANES)).reshape(value.shape)

    def build_spatial(turned):
        depth = 256
        return pl.pallas_call(
            functools.partial(spatial_build_kernel, turned),
            out_shape=pltpu.HBM((half_cells, half_cells), bf16),
            grid=(half_cells // depth,),
            in_specs=[smem, pl.BlockSpec((2, cell_count), lambda i: (0, 0))],
            out_specs=pl.BlockSpec((depth, half_cells), lambda i: (i, 0)),
            scratch_shapes=[pltpu.VMEM((16, half_cells), bf16)] * 2,
            compiler_params=small,
            name="spatial_build",
        )(half, coords)

    def spatial_step(received, kept):
        scratch = [pltpu.VMEM((rows, half_cells), f32), pltpu.VMEM((rows, cell_count), f32)]
        outputs = [pltpu.VMEM((rows, 2 * window), f32)]
        values, stored = (received,), ()
        if kept is None:
            count = cell_count // 512
            outputs.append(pltpu.VMEM((count, half_cells, 512), bf16))
            scratch.append(pltpu.SemaphoreType.DMA((count,)))
            stored = (own_spatial, other_spatial)
        else:
            values = (received, kept)
        results = call(
            functools.partial(spatial_kernel, block_count, kept is None),
            "spatial_step",
            (tiles, other_tiles),
            values,
            outputs,
            scratch,
            stored,
        )
        mine, kept = results if kept is None else (results, kept)
        return mine, from_other_half(mine), kept

    half = half_index.astype(jnp.int32).reshape(1)
    tiles = window_tiles.reshape(-1)
    other_probes = from_other_half(probes)
    other_tiles = from_other_half(tiles)
    own_probes, table, tile_rows, first_feet = call(
        prepare_kernel,
        "prepare",
        (),
        (),
        (
            pltpu.VMEM((rows, sound_count // 2), f32),
            pltpu.VMEM((2 * HALF_SUBLANES, LANES), f32),
            pltpu.VMEM((2 * HALF_SUBLANES, LANES), jnp.int32),
            pltpu.VMEM(footprints.shape, bf16),
        ),
        (
            pltpu.SMEM(tiles.shape, jnp.int32),
            pltpu.SMEM((top_count, block_count), jnp.int32),
            pltpu.SMEM((top_count, block_count), f32),
            pltpu.VMEM(probes.shape, f32),
            pltpu.SemaphoreType.DMA((5,)),
        ),
        (tiles, owners.T, lag_weights.T, probes, footprints),
    )
    to_mix, all_probes = call(
        start_kernel,
        "start",
        (half,),
        (own_probes, other_probes, table, tile_rows, first_feet, other_tiles),
        (pltpu.VMEM((periods * 2 * HALF_SUBLANES, LANES), bf16), vectors),
    )
    later_feet, to_mix = lax.optimization_barrier((footprints, to_mix))
    other_feet = from_other_half(later_feet)
    own_spatial = build_spatial(False)
    received, own_spatial = lax.optimization_barrier((send(to_mix), own_spatial))
    mixed, choice = call(
        functools.partial(first_mix_kernel, top_count),
        "first_mix",
        (),
        (received, temporal),
        (wire, pltpu.VMEM((4 * periods, periods * HALF_SUBLANES), bf16)),
        [pltpu.VMEM((periods * HALF_SUBLANES, LANES), f32)] * 2,
    )
    other_spatial = build_spatial(True)
    mine, theirs, kept = spatial_step(send(mixed), None)
    to_mix, first = call(
        turn_kernel,
        "turn",
        (),
        (mine, theirs, footprints, other_feet, tile_rows),
        (wire, vectors),
    )
    mixed = call(mix_kernel, "second_mix", (), (send(to_mix), temporal, choice), (wire,))
    mine, theirs, kept = spatial_step(send(mixed), kept)
    sums, second = call(
        functools.partial(last_kernel, probe_count),
        "last",
        (),
        (mine, theirs, footprints, other_feet, all_probes, first),
        (pltpu.VMEM((periods, LANES), f32), vectors),
    )
    sums = exchange(sums.reshape(periods, 1, LANES)).reshape(periods, LANES)
    return pl.pallas_call(
        functools.partial(finish_kernel, total_rows),
        out_shape=(
            jax.ShapeDtypeStruct((4, probe_count), f32),
            jax.ShapeDtypeStruct(probes.shape, f32),
        ),
        in_specs=[smem, vmem, vmem, vmem, vmem],
        out_specs=(vmem, vmem),
        compiler_params=small,
        name="finish",
    )(half, in_vmem(sums), in_vmem(all_probes), in_vmem(first), in_vmem(second))


def solution(mesh):
    in_specs = (
        P("period", None, "half"),
        P("period", None, "half"),
        P("period", None),
        P("period", None),
        P("period", "half"),
        P(),
        P(),
    )
    out_specs = (P(), P("period", None, "half"))
    return jax.shard_map(body, mesh=mesh, in_specs=in_specs, out_specs=out_specs, check_vma=False)
```

```python
import functools

import jax
import jax.numpy as jnp
from jax import lax
from jax.experimental import pallas as pl
from jax.experimental.pallas import tpu as pltpu
from jax.sharding import PartitionSpec as P


epsilon = 1e-06
kernel_scale = 0.05
kernel_length = 6.0
log2e = 1.4426950408889634
LANES = 128
HALF_LANES = 64
HALF_SUBLANES = 4
GROUP = 48


smem = pl.BlockSpec(memory_space=pltpu.SMEM)
vmem = pl.BlockSpec(memory_space=pltpu.VMEM)
hbm = pl.BlockSpec(memory_space=pltpu.HBM)
small = pltpu.CompilerParams(vmem_limit_bytes=24 * 1024 * 1024)


def in_hbm(value):
    return pltpu.with_memory_space_constraint(value, pltpu.HBM)


def in_vmem(value):
    return pltpu.with_memory_space_constraint(value, pltpu.VMEM)


def from_other_half(value):
    return lax.ppermute(value, "half", [(0, 1), (1, 0)])


def exchange(value):
    return lax.all_to_all(value, "period", split_axis=0, concat_axis=0, tiled=True)


def block_of_row(shape, block_count):
    return lax.rem(lax.broadcasted_iota(jnp.int32, shape, 0), block_count)


def halves(value):
    high = value.astype(jnp.bfloat16)
    low = (value - high.astype(jnp.float32)).astype(jnp.bfloat16)
    return high, low


def dot(left, right, dims=((1,), (0,))):
    return lax.dot_general(left, right, (dims, ((), ())), preferred_element_type=jnp.float32)


def tile_iotas():
    row = lax.broadcasted_iota(jnp.int32, (2 * HALF_SUBLANES, LANES), 0)
    lane = lax.broadcasted_iota(jnp.int32, (2 * HALF_SUBLANES, LANES), 1)
    return row, lane


def half_turn(tile):
    return pltpu.roll(tile, HALF_SUBLANES, 0)


def swap_quarters(tile):
    row, lane = tile_iotas()
    turned = half_turn(pltpu.roll(tile, HALF_LANES, 1))
    return jnp.where((row < HALF_SUBLANES) == (lane < HALF_LANES), tile, turned)


def group_span(group):
    return divmod(GROUP * group, LANES)


def pack_groups(tiles):
    row, lane = tile_iotas()
    left = lane < HALF_LANES
    diagonal = (row < HALF_SUBLANES) == left
    packed = []
    for pair in range(4):
        first, second = [], []
        for group in (2 * pair, 2 * pair + 1):
            place, at = group_span(group)
            source = tiles[place]
            if at + GROUP > LANES:
                source = jnp.where(lane >= at, source, tiles[place + 1])
            for target, end in ((first, 0), (second, HALF_LANES)):
                shift = (end - at) % LANES
                target.append(pltpu.roll(source, shift, 1) if shift else source)
        kept = jnp.where(left, first[0], second[1])
        moved = half_turn(jnp.where(left, first[1], second[0]))
        packed.append(jnp.where(diagonal, kept, moved))
    return packed


def unpack_groups(packed):
    row, lane = tile_iotas()
    upper = row < HALF_SUBLANES
    groups = []
    for tile in packed:
        turned = pltpu.roll(tile, HALF_LANES, 1)
        groups.append(jnp.where(upper, tile, half_turn(turned)))
        groups.append(jnp.where(upper, half_turn(tile), turned))
    tiles = [None, None, None]
    for group, value in enumerate(groups):
        place, at = group_span(group)
        value = pltpu.roll(value, at, 1) if at else value
        tiles[place] = value if at == 0 else jnp.where(lane >= at, value, tiles[place])
        if at + GROUP > LANES:
            tiles[place + 1] = value
    return tiles


def adjoint_pieces(vector, feet_ref):
    block_count, _, window = feet_ref.shape
    block_index = block_of_row((vector.shape[0], window), block_count)
    pieces = jnp.zeros((vector.shape[0], window), jnp.float32)
    for block in range(block_count):
        pieces = jnp.where(block_index == block, dot(vector, feet_ref[block]), pieces)
    return pieces


def placed_tile(pieces, tile_rows, tile, probe, probe_count):
    count = pieces.shape[0] // probe_count
    rows = slice(probe * count, (probe + 1) * count)
    value = jnp.where(tile_rows == tile, pieces[rows, :LANES], 0.0)
    return jnp.where(tile_rows == tile - 1, pieces[rows, LANES:], value)


def distance_terms(cells, turned):
    x, y = cells[0:1], cells[1:2]
    norm = x * x + y * y
    low = (norm & 255).astype(jnp.float32)
    high = (norm - (norm & 255)).astype(jnp.float32)
    x, y, one = x.astype(jnp.float32), y.astype(jnp.float32), jnp.ones(x.shape, jnp.float32)
    if turned:
        terms = [-2.0 * x, -2.0 * y, one, one, high, low]
    else:
        terms = [x, y, high, low, one, one]
    row = lax.broadcasted_iota(jnp.int32, (16, x.shape[1]), 0)
    result = jnp.zeros((16, x.shape[1]), jnp.float32)
    for place, term in enumerate(terms):
        result = jnp.where(row == place, term, result)
    return result.astype(jnp.bfloat16)


def prepare_kernel(tiles_in, owners_in, weights_in, own_in, coords_in, feet_in, own_ref, table_ref, tile_rows_ref, left_ref, right_ref, feet_ref, tiles_ref, owners_ref, weights_ref, probes_ref, coords_ref, sems):
    block_count, probe_count, _ = probes_ref.shape
    top_count = owners_ref.shape[0]
    pairs = (
        (tiles_in, tiles_ref),
        (owners_in, owners_ref),
        (weights_in, weights_ref),
        (own_in, probes_ref),
        (coords_in, coords_ref),
        (feet_in, feet_ref),
    )
    copies = [
        pltpu.make_async_copy(source, target, sems.at[place])
        for place, (source, target) in enumerate(pairs)
    ]
    for copy in copies:
        copy.start()
    for copy in copies[:5]:
        copy.wait()
    for probe in range(probe_count):
        rows = slice(probe * block_count, (probe + 1) * block_count)
        own_ref[rows, :] = probes_ref[:, probe, :]
    row, lane = tile_iotas()
    owner = jnp.zeros(row.shape, jnp.float32)
    weight = jnp.zeros(row.shape, jnp.float32)
    for block in range(block_count):
        column, turn = divmod(block, HALF_SUBLANES)
        for top in range(top_count):
            here = lane == column * HALF_LANES + GROUP + top
            here = here & (lax.rem(row, HALF_SUBLANES) == turn)
            owner = jnp.where(here, owners_ref[top, block].astype(jnp.float32), owner)
            weight = jnp.where(here, weights_ref[top, block], weight)
    table = owner
    for part in range(1, 4):
        high = weight.astype(jnp.bfloat16).astype(jnp.float32)
        table = table + pltpu.roll(high, part * top_count, 1)
        weight = weight - high
    table_ref[...] = table
    tile_rows = jnp.zeros(row.shape, jnp.int32)
    for block in range(block_count):
        tile_rows = jnp.where(row == block, tiles_ref[block], tile_rows)
    tile_rows_ref[...] = tile_rows
    half = lax.axis_index("half")
    half_cells = left_ref.shape[1]
    own_at = pl.multiple_of(half * half_cells, LANES)
    other_at = pl.multiple_of((1 - half) * half_cells, LANES)
    own = coords_ref[:, pl.ds(own_at, half_cells)]
    left_ref[...] = distance_terms(own, False)
    right_ref[:, :half_cells] = distance_terms(own, True)
    right_ref[:, half_cells:] = distance_terms(coords_ref[:, pl.ds(other_at, half_cells)], True)
    copies[5].wait()


def start_kernel(own_ref, other_ref, table_ref, tile_rows_ref, feet_ref, others_ref, out_ref, probes_ref, other_rows_ref):
    half = lax.axis_index("half")
    block_count, probe_count, half_sound = other_ref.shape
    own_at = pl.multiple_of(half * half_sound, LANES)
    other_at = pl.multiple_of((1 - half) * half_sound, LANES)
    probes_ref[:, pl.ds(own_at, half_sound)] = own_ref[...]
    for probe in range(probe_count):
        rows = slice(probe * block_count, (probe + 1) * block_count)
        probes_ref[rows, pl.ds(other_at, half_sound)] = other_ref[:, probe, :]
    square = (block_count, block_count)
    on_diagonal = lax.broadcasted_iota(jnp.int32, square, 0) == lax.broadcasted_iota(
        jnp.int32, square, 1
    )
    others = jnp.where(on_diagonal, jnp.broadcast_to(others_ref[...], square), 0)
    others = jnp.sum(others, axis=1, keepdims=True)
    other_rows_ref[...] = jnp.broadcast_to(others, other_rows_ref.shape)
    pieces = adjoint_pieces(probes_ref[...].astype(jnp.bfloat16), feet_ref)
    table, tile_rows = table_ref[...], tile_rows_ref[...]
    _, lane = tile_iotas()
    data = lax.rem(lane, HALF_LANES) < GROUP
    size = 2 * block_count
    triples = out_ref.shape[0] // (2 * size * probe_count)
    for probe in range(probe_count):
        for triple in range(triples):
            packed = pack_groups(
                [
                    placed_tile(pieces, tile_rows, 3 * triple + part, probe, probe_count)
                    for part in range(3)
                ]
            )
            packed = [jnp.where(data, tile, table) for tile in packed]
            at = 2 * size * (probe * triples + triple)
            for part in range(2):
                out_ref[at + part * size : at + (part + 1) * size, :] = jnp.concatenate(
                    packed[2 * part : 2 * part + 2], axis=0
                ).astype(jnp.bfloat16)


def spatial_build_kernel(left_ref, right_ref, out_ref):
    squared = jnp.maximum(dot(left_ref[...], right_ref[...], ((0,), (0,))), 1e-12)
    distance = squared * lax.rsqrt(squared)
    out_ref[...] = jnp.exp2(distance * (-log2e / kernel_length)).astype(jnp.bfloat16)


def mix(received, choice, temporal):
    periods = temporal.shape[0]
    both = dot(choice, received)
    both = both[: 2 * periods] + both[2 * periods :]
    gathered = both[:periods] + pltpu.roll(both[periods:], HALF_LANES, 1)
    mixed = lax.dot_general(
        gathered * kernel_scale,
        temporal,
        (((0,), (1,)), ((), ())),
        precision=lax.Precision.HIGHEST,
        preferred_element_type=jnp.float32,
    )
    high, low = halves(mixed[:HALF_LANES])

    def columns(part):
        nothing = jnp.zeros(part.shape, part.dtype)
        upper = jnp.concatenate([part, nothing], axis=1)
        return jnp.concatenate([upper, jnp.concatenate([nothing, part], axis=1)], axis=0)

    high, low = columns(high), columns(low)
    upper, lower = choice[: 2 * periods], choice[2 * periods :]
    return (dot(high, upper) + dot(high, lower) + dot(low, upper)).T.astype(jnp.bfloat16)


def first_mix_kernel(top_count, received_ref, temporal_ref, out_ref, choice_ref):
    periods = temporal_ref.shape[0]
    wide = received_ref[...].astype(jnp.float32).T
    shape = (periods, wide.shape[1])
    period = lax.broadcasted_iota(jnp.int32, shape, 0).astype(jnp.float32)
    for column in range(2):
        choice = jnp.zeros(shape, jnp.float32)
        for top in range(top_count):
            at = column * HALF_LANES + GROUP + top
            owner = wide[at : at + 1]
            weight = (
                wide[at + top_count : at + top_count + 1]
                + wide[at + 2 * top_count : at + 2 * top_count + 1]
                + wide[at + 3 * top_count : at + 3 * top_count + 1]
            )
            choice = choice + jnp.where(owner == period, weight, 0.0)
        high, low = halves(choice)
        choice_ref[column * periods : (column + 1) * periods, :] = high
        choice_ref[(2 + column) * periods : (3 + column) * periods, :] = low
    out_ref[...] = mix(received_ref[...], choice_ref[...], temporal_ref[...])


def mix_kernel(received_ref, temporal_ref, choice_ref, out_ref):
    out_ref[...] = mix(received_ref[...], choice_ref[...], temporal_ref[...])


def spatial_kernel(block_count, chunks, streamed, received_ref, tile_rows_ref, other_rows_ref, *refs):
    if streamed:
        own_spatial, other_spatial, out_ref, kept_ref, field, total, sems = refs
    else:
        kept_ref, out_ref, field, total = refs
    rows, half_cells = field.shape
    probe_count = rows // block_count
    tile_count = half_cells // LANES
    copies = []
    if streamed:
        sides = (own_spatial, other_spatial)
        copies = [
            pltpu.make_async_copy(
                sides[side].at[:, start:end], kept_ref.at[side, :, start:end], sems.at[place]
            )
            for place, (side, start, end) in enumerate(chunks)
        ]
        for copy in copies:
            copy.start()
    size = 2 * block_count

    def unpack(probe, carry):
        into = pl.multiple_of(probe * block_count, block_count)
        for triple in range(tile_count // 3):
            at = pl.multiple_of(2 * size * (probe * (tile_count // 3) + triple), size)
            both = received_ref[pl.ds(at, 2 * size), :].astype(jnp.float32)
            packed = [both[part * block_count : (part + 1) * block_count] for part in range(4)]
            for part, value in enumerate(unpack_groups(packed)):
                start = (3 * triple + part) * LANES
                field[pl.ds(into, block_count), start : start + LANES] = value
        return carry

    if streamed:
        lax.fori_loop(0, probe_count, unpack, 0)
    else:
        for pair in range(tile_count * probe_count // 2):
            both = received_ref[size * pair : size * (pair + 1), :].astype(jnp.float32)
            for part in range(2):
                tile, probe = divmod(2 * pair + part, probe_count)
                field[
                    probe * block_count : (probe + 1) * block_count,
                    tile * LANES : (tile + 1) * LANES,
                ] = swap_quarters(both[part * block_count : (part + 1) * block_count])
    cells = field[...].astype(jnp.bfloat16)
    for place, (side, start, end) in enumerate(chunks):
        if streamed:
            copies[place].wait()
        at = side * half_cells
        total[:, at + start : at + end] = dot(cells, kept_ref[side, :, start:end])
    nothing = jnp.zeros((block_count, LANES), jnp.float32)
    for side, rows_ref in enumerate((tile_rows_ref, other_rows_ref)):
        first_tile = rows_ref[...]
        for probe in range(probe_count):
            rows_of = slice(probe * block_count, (probe + 1) * block_count)
            window = [nothing, nothing]
            for tile in range(tile_count):
                at = side * half_cells + tile * LANES
                values = total[rows_of, at : at + LANES]
                for part in range(2):
                    window[part] = jnp.where(first_tile == tile - part, values, window[part])
            for part in range(2):
                at = (2 * side + part) * LANES
                out_ref[rows_of, at : at + LANES] = window[part]


def sound(mine_ref, theirs_ref, feet_ref, other_feet_ref):
    block_count, sound_count, window = feet_ref.shape
    rows = mine_ref.shape[0]
    own = (mine_ref[:, :window] + theirs_ref[:, window:]).astype(jnp.bfloat16)
    other = (mine_ref[:, window:] + theirs_ref[:, :window]).astype(jnp.bfloat16)
    block_index = block_of_row((rows, sound_count), block_count)
    image = jnp.zeros((rows, sound_count), jnp.float32)
    for block in range(block_count):
        part = dot(own, feet_ref[block], ((1,), (1,)))
        part = part + dot(other, other_feet_ref[block], ((1,), (1,)))
        image = jnp.where(block_index == block, part, image)
    return image


def turn_kernel(mine_ref, theirs_ref, feet_ref, other_feet_ref, tile_rows_ref, out_ref, image_ref):
    image = sound(mine_ref, theirs_ref, feet_ref, other_feet_ref)
    image_ref[...] = image
    pieces = adjoint_pieces(image.astype(jnp.bfloat16), feet_ref)
    tile_rows = tile_rows_ref[...]
    size = 2 * feet_ref.shape[0]
    probe_count = image.shape[0] // feet_ref.shape[0]
    count = out_ref.shape[0] // size * 3 // 4
    for pair in range(count):
        tiles = [
            swap_quarters(
                placed_tile(pieces, tile_rows, *divmod(2 * pair + part, probe_count), probe_count)
            )
            for part in range(2)
        ]
        out_ref[size * pair : size * (pair + 1), :] = jnp.concatenate(tiles, axis=0).astype(
            jnp.bfloat16
        )
    out_ref[size * count :, :] = jnp.zeros((out_ref.shape[0] - size * count, LANES), jnp.bfloat16)


def last_kernel(probe_count, mine_ref, theirs_ref, feet_ref, other_feet_ref, probes_ref, first_ref, sums_ref, second_ref):
    second = sound(mine_ref, theirs_ref, feet_ref, other_feet_ref)
    second_ref[...] = second
    probes = probes_ref[...]
    first = first_ref[...]
    block_count = second.shape[0] // probe_count
    lane = lax.broadcasted_iota(jnp.int32, (1, LANES), 1)
    row = jnp.zeros((1, LANES), jnp.float32)
    pairs = (
        (probes, probes),
        (probes, first),
        (first, first),
        (probes, second),
        (first, second),
        (second, second),
    )
    for place, (left, right) in enumerate(pairs):
        product = left * right
        for probe in range(probe_count):
            value = jnp.sum(
                product[probe * block_count : (probe + 1) * block_count], axis=0, keepdims=True
            )
            value = jnp.sum(value, axis=1, keepdims=True)
            row = jnp.where(lane == place * probe_count + probe, value, row)
    sums_ref[...] = jnp.broadcast_to(row, sums_ref.shape)


def finish_kernel(total_rows, sums_ref, probes_ref, first_ref, second_ref, coefficients_ref, residual_ref):
    block_count, probe_count, half_sound = residual_ref.shape
    row = jnp.sum(sums_ref[...], axis=0, keepdims=True) / total_rows

    def stat(place):
        shift = (LANES - place * probe_count) % LANES
        return row if shift == 0 else pltpu.roll(row, shift, 1)

    pp, pw, ww, px, wx, xx = [stat(place) for place in range(6)]
    scale_square = pp + epsilon
    scale = jnp.sqrt(scale_square)
    alpha_one = pw / scale_square
    rest = (ww - 2.0 * alpha_one * pw + alpha_one * alpha_one * pp) / scale_square
    beta_one = jnp.sqrt(jnp.maximum(rest, 0.0) + epsilon)
    cross = wx - alpha_one * ww - alpha_one * px + alpha_one * alpha_one * pw
    alpha_two = (cross / (beta_one * beta_one) - (pw - alpha_one * pp)) / scale_square
    of_second = 1.0 / (scale * beta_one)
    of_first = -(alpha_one + alpha_two) * of_second
    of_probes = (alpha_one * alpha_two / beta_one - beta_one) / scale
    square = (
        of_second * of_second * xx
        + of_first * of_first * ww
        + of_probes * of_probes * pp
        + 2.0 * (of_second * of_first * wx + of_second * of_probes * px + of_first * of_probes * pw)
    )
    beta_two = jnp.sqrt(jnp.maximum(square, 0.0) + epsilon)
    for place, value in enumerate((alpha_one, beta_one, alpha_two, beta_two)):
        coefficients_ref[place : place + 1, :] = value[:, :probe_count]
    at = pl.multiple_of(lax.axis_index("half") * half_sound, LANES)
    for probe in range(probe_count):
        rows = slice(probe * block_count, (probe + 1) * block_count)
        residual_ref[:, probe, :] = (
            of_second[:, probe : probe + 1] * second_ref[rows, pl.ds(at, half_sound)]
            + of_first[:, probe : probe + 1] * first_ref[rows, pl.ds(at, half_sound)]
            + of_probes[:, probe : probe + 1] * probes_ref[rows, pl.ds(at, half_sound)]
        )


def body(probes, footprints, lag_weights, owners, window_tiles, coords, temporal):
    periods = lax.axis_size("period")
    block_count, top_count = owners.shape
    probe_count = probes.shape[1]
    sound_count = footprints.shape[1]
    window = footprints.shape[2]
    cell_count = coords.shape[1]
    half_cells = cell_count // 2
    rows = block_count * probe_count
    total_rows = float(block_count * periods * sound_count)
    f32, bf16 = jnp.float32, jnp.bfloat16
    wire = pltpu.VMEM((periods * HALF_SUBLANES, LANES), bf16)
    vectors = pltpu.VMEM((rows, sound_count), f32)

    def call(kernel, scalars, values, outputs, scratch=(), left_in_hbm=()):
        outputs = tuple(outputs)
        results = pl.pallas_call(
            kernel,
            out_shape=outputs,
            in_specs=[smem] * len(scalars) + [vmem] * len(values) + [hbm] * len(left_in_hbm),
            out_specs=tuple(vmem for _ in outputs),
            scratch_shapes=list(scratch),
            compiler_params=small,
        )(
            *scalars,
            *[in_vmem(value) for value in values],
            *[in_hbm(value) for value in left_in_hbm],
        )
        return results if len(outputs) > 1 else results[0]

    def send(value):
        count = value.shape[0] // periods
        return exchange(value.reshape(periods, count, LANES)).reshape(value.shape)

    def build_spatial(side):
        depth = 256
        return pl.pallas_call(
            spatial_build_kernel,
            out_shape=pltpu.HBM((half_cells, half_cells), bf16),
            grid=(half_cells // depth,),
            in_specs=[
                pl.BlockSpec((16, depth), lambda i: (0, i)),
                pl.BlockSpec((16, half_cells), lambda i: (0, side)),
            ],
            out_specs=pl.BlockSpec((depth, half_cells), lambda i: (i, 0)),
            compiler_params=small,
            name="spatial_build",
        )(in_vmem(left), in_vmem(right))

    chunks = ((0, 0, 1024), (0, 1024, 1536), (1, 0, 512), (1, 512, 1024), (1, 1024, 1536))

    def spatial_step(received, kept):
        scratch = [pltpu.VMEM((rows, half_cells), f32), pltpu.VMEM((rows, cell_count), f32)]
        outputs = [pltpu.VMEM((rows, 2 * window), f32)]
        values, stored = (received, tile_rows, other_rows), ()
        if kept is None:
            outputs.append(pltpu.VMEM((2, half_cells, half_cells), bf16))
            scratch.append(pltpu.SemaphoreType.DMA((len(chunks),)))
            stored = (own_spatial, other_spatial)
        else:
            values = values + (kept,)
        results = call(
            functools.partial(spatial_kernel, block_count, chunks, kept is None),
            (),
            values,
            outputs,
            scratch,
            stored,
        )
        mine, kept = results if kept is None else (results, kept)
        return mine, from_other_half(mine), kept

    tiles = window_tiles.reshape(-1)
    other_probes = from_other_half(probes)
    other_tiles = from_other_half(tiles)
    own_probes, table, tile_rows, left, right, first_feet = call(
        prepare_kernel,
        (),
        (),
        (
            pltpu.VMEM((rows, sound_count // 2), f32),
            pltpu.VMEM((2 * HALF_SUBLANES, LANES), f32),
            pltpu.VMEM((2 * HALF_SUBLANES, LANES), jnp.int32),
            pltpu.VMEM((16, half_cells), bf16),
            pltpu.VMEM((16, cell_count), bf16),
            pltpu.VMEM(footprints.shape, bf16),
        ),
        (
            pltpu.SMEM(tiles.shape, jnp.int32),
            pltpu.SMEM((top_count, block_count), jnp.int32),
            pltpu.SMEM((top_count, block_count), f32),
            pltpu.VMEM(probes.shape, f32),
            pltpu.VMEM(coords.shape, jnp.int32),
            pltpu.SemaphoreType.DMA((6,)),
        ),
        (tiles, owners.T, lag_weights.T, probes, coords, footprints),
    )
    to_mix, all_probes, other_rows = call(
        start_kernel,
        (),
        (own_probes, other_probes, table, tile_rows, first_feet, other_tiles.reshape(1, -1)),
        (wire, vectors, pltpu.VMEM((block_count, LANES), jnp.int32)),
    )
    received = send(to_mix)
    other_feet = from_other_half(footprints)
    own_spatial = build_spatial(0)
    received, own_spatial = lax.optimization_barrier((received, own_spatial))
    mixed, choice = call(
        functools.partial(first_mix_kernel, top_count),
        (),
        (received, temporal),
        (wire, pltpu.VMEM((4 * periods, periods * HALF_SUBLANES), bf16)),
    )
    other_spatial = build_spatial(1)
    mine, theirs, kept = spatial_step(send(mixed), None)
    to_mix, first = call(
        turn_kernel, (), (mine, theirs, footprints, other_feet, tile_rows), (wire, vectors)
    )
    mixed = call(mix_kernel, (), (send(to_mix), temporal, choice), (wire,))
    mine, theirs, kept = spatial_step(send(mixed), kept)
    sums, second = call(
        functools.partial(last_kernel, probe_count),
        (),
        (mine, theirs, footprints, other_feet, all_probes, first),
        (pltpu.VMEM((periods, LANES), f32), vectors),
    )
    sums = exchange(sums.reshape(periods, 1, LANES)).reshape(periods, LANES)
    return pl.pallas_call(
        functools.partial(finish_kernel, total_rows),
        out_shape=(
            jax.ShapeDtypeStruct((4, probe_count), f32),
            jax.ShapeDtypeStruct(probes.shape, f32),
        ),
        in_specs=[vmem, vmem, vmem, vmem],
        out_specs=(vmem, vmem),
        compiler_params=small,
        name="finish",
    )(in_vmem(sums), in_vmem(all_probes), in_vmem(first), in_vmem(second))


def solution(mesh):
    in_specs = (
        P("period", None, "half"),
        P("period", None, "half"),
        P("period", None),
        P("period", None),
        P("period", "half"),
        P(),
        P(),
    )
    out_specs = (P(), P("period", None, "half"))
    return jax.shard_map(body, mesh=mesh, in_specs=in_specs, out_specs=out_specs, check_vma=False)
```

```python
import functools

import jax
import jax.numpy as jnp
from jax import lax
from jax.experimental import pallas as pl
from jax.experimental.pallas import tpu as pltpu
from jax.sharding import PartitionSpec as P


epsilon = 1e-06
kernel_scale = 0.05
kernel_length = 6.0
log2e = 1.4426950408889634
LANES = 128
HALF_LANES = 64
HALF_SUBLANES = 4
GROUP = 48


smem = pl.BlockSpec(memory_space=pltpu.SMEM)
vmem = pl.BlockSpec(memory_space=pltpu.VMEM)
hbm = pl.BlockSpec(memory_space=pltpu.HBM)
small = pltpu.CompilerParams(vmem_limit_bytes=24 * 1024 * 1024)


def in_hbm(value):
    return pltpu.with_memory_space_constraint(value, pltpu.HBM)


def in_vmem(value):
    return pltpu.with_memory_space_constraint(value, pltpu.VMEM)


def from_other_half(value):
    return lax.ppermute(value, "half", [(0, 1), (1, 0)])


def exchange(value):
    return lax.all_to_all(value, "period", split_axis=0, concat_axis=0, tiled=True)


def block_of_row(shape, block_count):
    return lax.rem(lax.broadcasted_iota(jnp.int32, shape, 0), block_count)


def halves(value):
    high = value.astype(jnp.bfloat16)
    low = (value - high.astype(jnp.float32)).astype(jnp.bfloat16)
    return high, low


def dot(left, right, dims=((1,), (0,))):
    return lax.dot_general(left, right, (dims, ((), ())), preferred_element_type=jnp.float32)


def tile_iotas():
    row = lax.broadcasted_iota(jnp.int32, (2 * HALF_SUBLANES, LANES), 0)
    lane = lax.broadcasted_iota(jnp.int32, (2 * HALF_SUBLANES, LANES), 1)
    return row, lane


def half_turn(tile):
    return pltpu.roll(tile, HALF_SUBLANES, 0)


def swap_quarters(tile):
    row, lane = tile_iotas()
    turned = half_turn(pltpu.roll(tile, HALF_LANES, 1))
    return jnp.where((row < HALF_SUBLANES) == (lane < HALF_LANES), tile, turned)


def group_span(group):
    return divmod(GROUP * group, LANES)


def pack_groups(tiles):
    row, lane = tile_iotas()
    left = lane < HALF_LANES
    diagonal = (row < HALF_SUBLANES) == left
    packed = []
    for pair in range(4):
        first, second = [], []
        for group in (2 * pair, 2 * pair + 1):
            place, at = group_span(group)
            source = tiles[place]
            if at + GROUP > LANES:
                source = jnp.where(lane >= at, source, tiles[place + 1])
            for target, end in ((first, 0), (second, HALF_LANES)):
                shift = (end - at) % LANES
                target.append(pltpu.roll(source, shift, 1) if shift else source)
        kept = jnp.where(left, first[0], second[1])
        moved = half_turn(jnp.where(left, first[1], second[0]))
        packed.append(jnp.where(diagonal, kept, moved))
    return packed


def unpack_groups(packed):
    row, lane = tile_iotas()
    upper = row < HALF_SUBLANES
    groups = []
    for tile in packed:
        turned = pltpu.roll(tile, HALF_LANES, 1)
        groups.append(jnp.where(upper, tile, half_turn(turned)))
        groups.append(jnp.where(upper, half_turn(tile), turned))
    tiles = [None, None, None]
    for group, value in enumerate(groups):
        place, at = group_span(group)
        value = pltpu.roll(value, at, 1) if at else value
        tiles[place] = value if at == 0 else jnp.where(lane >= at, value, tiles[place])
        if at + GROUP > LANES:
            tiles[place + 1] = value
    return tiles


def adjoint_pieces(vector, feet_ref):
    block_count, _, window = feet_ref.shape
    block_index = block_of_row((vector.shape[0], window), block_count)
    pieces = jnp.zeros((vector.shape[0], window), jnp.float32)
    for block in range(block_count):
        pieces = jnp.where(block_index == block, dot(vector, feet_ref[block]), pieces)
    return pieces


def placed_tile(pieces, tile_rows, tile, probe, probe_count):
    count = pieces.shape[0] // probe_count
    rows = slice(probe * count, (probe + 1) * count)
    value = jnp.where(tile_rows == tile, pieces[rows, :LANES], 0.0)
    return jnp.where(tile_rows == tile - 1, pieces[rows, LANES:], value)


def distance_terms(cells, turned):
    x, y = cells[0:1], cells[1:2]
    norm = x * x + y * y
    low = (norm & 255).astype(jnp.float32)
    high = (norm - (norm & 255)).astype(jnp.float32)
    x, y, one = x.astype(jnp.float32), y.astype(jnp.float32), jnp.ones(x.shape, jnp.float32)
    if turned:
        terms = [-2.0 * x, -2.0 * y, one, one, high, low]
    else:
        terms = [x, y, high, low, one, one]
    row = lax.broadcasted_iota(jnp.int32, (16, x.shape[1]), 0)
    result = jnp.zeros((16, x.shape[1]), jnp.float32)
    for place, term in enumerate(terms):
        result = jnp.where(row == place, term, result)
    return result.astype(jnp.bfloat16)


def prepare_kernel(tiles_in, owners_in, weights_in, own_in, coords_in, feet_in, own_ref, table_ref, tile_rows_ref, left_ref, right_ref, feet_ref, tiles_ref, owners_ref, weights_ref, probes_ref, coords_ref, sems):
    block_count, probe_count, _ = probes_ref.shape
    top_count = owners_ref.shape[0]
    pairs = (
        (tiles_in, tiles_ref),
        (owners_in, owners_ref),
        (weights_in, weights_ref),
        (own_in, probes_ref),
        (coords_in, coords_ref),
        (feet_in, feet_ref),
    )
    copies = [
        pltpu.make_async_copy(source, target, sems.at[place])
        for place, (source, target) in enumerate(pairs)
    ]
    for copy in copies:
        copy.start()
    for copy in copies[:5]:
        copy.wait()
    for probe in range(probe_count):
        rows = slice(probe * block_count, (probe + 1) * block_count)
        own_ref[rows, :] = probes_ref[:, probe, :]
    row, lane = tile_iotas()
    owner = jnp.zeros(row.shape, jnp.float32)
    weight = jnp.zeros(row.shape, jnp.float32)
    for block in range(block_count):
        column, turn = divmod(block, HALF_SUBLANES)
        for top in range(top_count):
            here = lane == column * HALF_LANES + GROUP + top
            here = here & (lax.rem(row, HALF_SUBLANES) == turn)
            owner = jnp.where(here, owners_ref[top, block].astype(jnp.float32), owner)
            weight = jnp.where(here, weights_ref[top, block], weight)
    table_ref[...] = owner + pltpu.roll(weight, top_count, 1)
    tile_rows = jnp.zeros(row.shape, jnp.int32)
    for block in range(block_count):
        tile_rows = jnp.where(row == block, tiles_ref[block], tile_rows)
    tile_rows_ref[...] = tile_rows
    half = lax.axis_index("half")
    half_cells = left_ref.shape[1]
    own_at = pl.multiple_of(half * half_cells, LANES)
    other_at = pl.multiple_of((1 - half) * half_cells, LANES)
    own = coords_ref[:, pl.ds(own_at, half_cells)]
    left_ref[...] = distance_terms(own, False)
    right_ref[:, :half_cells] = distance_terms(own, True)
    right_ref[:, half_cells:] = distance_terms(coords_ref[:, pl.ds(other_at, half_cells)], True)
    copies[5].wait()


def start_kernel(own_ref, other_ref, table_ref, tile_rows_ref, feet_ref, others_ref, out_ref, probes_ref, other_rows_ref):
    half = lax.axis_index("half")
    block_count, probe_count, half_sound = other_ref.shape
    own_at = pl.multiple_of(half * half_sound, LANES)
    other_at = pl.multiple_of((1 - half) * half_sound, LANES)
    probes_ref[:, pl.ds(own_at, half_sound)] = own_ref[...]
    for probe in range(probe_count):
        rows = slice(probe * block_count, (probe + 1) * block_count)
        probes_ref[rows, pl.ds(other_at, half_sound)] = other_ref[:, probe, :]
    square = (block_count, block_count)
    on_diagonal = lax.broadcasted_iota(jnp.int32, square, 0) == lax.broadcasted_iota(
        jnp.int32, square, 1
    )
    others = jnp.where(on_diagonal, jnp.broadcast_to(others_ref[...], square), 0)
    others = jnp.sum(others, axis=1, keepdims=True)
    other_rows_ref[...] = jnp.broadcast_to(others, other_rows_ref.shape)
    pieces = adjoint_pieces(probes_ref[...].astype(jnp.bfloat16), feet_ref)
    table, tile_rows = table_ref[...], tile_rows_ref[...]
    _, lane = tile_iotas()
    data = lax.rem(lane, HALF_LANES) < GROUP
    size = 2 * block_count
    triples = out_ref.shape[0] // (2 * size * probe_count)
    for probe in range(probe_count):
        for triple in range(triples):
            packed = pack_groups(
                [
                    placed_tile(pieces, tile_rows, 3 * triple + part, probe, probe_count)
                    for part in range(3)
                ]
            )
            packed = [jnp.where(data, tile, table) for tile in packed]
            at = 2 * size * (probe * triples + triple)
            for part in range(2):
                out_ref[at + part * size : at + (part + 1) * size, :] = jnp.concatenate(
                    packed[2 * part : 2 * part + 2], axis=0
                ).astype(jnp.bfloat16)


def spatial_values(left, right):
    squared = jnp.maximum(dot(left, right, ((0,), (0,))), 1e-12)
    distance = squared * lax.rsqrt(squared)
    return jnp.exp2(distance * (-log2e / kernel_length)).astype(jnp.bfloat16)


def first_build_kernel(left_ref, right_ref, own_out, top_out, buffers, sems):
    half_cells = left_ref.shape[1]
    depth = buffers.shape[1]
    count = half_cells // depth
    copies = []
    for place in range(count + 1):
        at = depth * (place % count)
        if place < count:
            right = right_ref[:, at:half_cells]
            target = own_out.at[at : at + depth, at:]
        else:
            right = right_ref[:, half_cells:]
            target = top_out
        buffers[place, :, at:] = spatial_values(left_ref[:, at : at + depth], right)
        copy = pltpu.make_async_copy(buffers.at[place, :, at:], target, sems.at[place])
        copy.start()
        copies.append(copy)
    for copy in copies:
        copy.wait()


def second_build_kernel(left_ref, right_ref, out_ref):
    out_ref[...] = spatial_values(left_ref[...], right_ref[...])


def mix(received, choice, temporal):
    periods = temporal.shape[0]
    both = dot(choice, received)
    gathered = both[:periods] + pltpu.roll(both[periods:], HALF_LANES, 1)
    high, low = halves(gathered * kernel_scale)
    temporal_high, temporal_low = halves(temporal)
    turned = ((0,), (1,))
    mixed = dot(high, temporal_high, turned) + dot(high, temporal_low, turned)
    mixed = (mixed + dot(low, temporal_high, turned))[:HALF_LANES].astype(jnp.bfloat16)
    nothing = jnp.zeros(mixed.shape, jnp.bfloat16)
    upper = jnp.concatenate([mixed, nothing], axis=1)
    lower = jnp.concatenate([nothing, mixed], axis=1)
    return dot(jnp.concatenate([upper, lower], axis=0), choice).T.astype(jnp.bfloat16)


def first_mix_kernel(top_count, received_ref, temporal_ref, out_ref, choice_ref):
    periods = temporal_ref.shape[0]
    wide = received_ref[...].astype(jnp.float32).T
    shape = (periods, wide.shape[1])
    period = lax.broadcasted_iota(jnp.int32, shape, 0).astype(jnp.float32)
    for column in range(2):
        choice = jnp.zeros(shape, jnp.float32)
        for top in range(top_count):
            at = column * HALF_LANES + GROUP + top
            weight = wide[at + top_count : at + top_count + 1]
            choice = jnp.where(wide[at : at + 1] == period, weight, choice)
        choice_ref[column * periods : (column + 1) * periods, :] = choice.astype(jnp.bfloat16)
    out_ref[...] = mix(received_ref[...], choice_ref[...], temporal_ref[...])


def mix_kernel(received_ref, temporal_ref, choice_ref, out_ref):
    out_ref[...] = mix(received_ref[...], choice_ref[...], temporal_ref[...])


def spatial_kernel(block_count, depth, width, streamed, received_ref, tile_rows_ref, other_rows_ref, *refs):
    if streamed:
        own_in, top_in, rest_in, feet_in, out_ref, kept_ref, feet_ref, field, total, sems = refs
    else:
        kept_ref, out_ref, field, total = refs
    rows, half_cells = field.shape
    probe_count = rows // block_count
    tile_count = half_cells // LANES
    own_copies, other_copies = [], []
    if streamed:
        pairs = [
            (own_in.at[at : at + depth, at:], kept_ref.at[0, at : at + depth, at:])
            for at in range(0, half_cells, depth)
        ]
        for at in range(0, half_cells, width):
            columns = slice(at, at + width)
            pairs.append((top_in.at[:, columns], kept_ref.at[1, :depth, columns]))
            pairs.append((rest_in.at[:, columns], kept_ref.at[1, depth:, columns]))
        pairs.append((feet_in, feet_ref))
        copies = [
            pltpu.make_async_copy(source, target, sems.at[place])
            for place, (source, target) in enumerate(pairs)
        ]
        for copy in copies:
            copy.start()
        own_copies, other_copies = copies[: half_cells // depth], copies[half_cells // depth :]
        feet_copy = copies[-1]
    size = 2 * block_count

    def unpack(probe, carry):
        into = pl.multiple_of(probe * block_count, block_count)
        for triple in range(tile_count // 3):
            at = pl.multiple_of(2 * size * (probe * (tile_count // 3) + triple), size)
            both = received_ref[pl.ds(at, 2 * size), :].astype(jnp.float32)
            packed = [both[part * block_count : (part + 1) * block_count] for part in range(4)]
            for part, value in enumerate(unpack_groups(packed)):
                start = (3 * triple + part) * LANES
                field[pl.ds(into, block_count), start : start + LANES] = value
        return carry

    if streamed:
        lax.fori_loop(0, probe_count, unpack, 0)
    else:
        for pair in range(tile_count * probe_count // 2):
            both = received_ref[size * pair : size * (pair + 1), :].astype(jnp.float32)
            for part in range(2):
                tile, probe = divmod(2 * pair + part, probe_count)
                field[
                    probe * block_count : (probe + 1) * block_count,
                    tile * LANES : (tile + 1) * LANES,
                ] = swap_quarters(both[part * block_count : (part + 1) * block_count])
    cells = field[...].astype(jnp.bfloat16)
    for copy in own_copies:
        copy.wait()
    for at in range(0, half_cells, depth):
        end = at + depth
        value = dot(cells[:, :end], kept_ref[0, :end, at:end])
        if end < half_cells:
            value = value + dot(cells[:, end:], kept_ref[0, at:end, end:], ((1,), (1,)))
        total[:, at:end] = value
    for place, at in enumerate(range(0, half_cells, width)):
        for copy in other_copies[2 * place : 2 * place + 2]:
            copy.wait()
        start = half_cells + at
        total[:, start : start + width] = dot(cells, kept_ref[1, :, at : at + width])
    nothing = jnp.zeros((block_count, LANES), jnp.float32)
    for side, rows_ref in enumerate((tile_rows_ref, other_rows_ref)):
        first_tile = rows_ref[...]
        for probe in range(probe_count):
            rows_of = slice(probe * block_count, (probe + 1) * block_count)
            window = [nothing, nothing]
            for tile in range(tile_count):
                at = side * half_cells + tile * LANES
                values = total[rows_of, at : at + LANES]
                for part in range(2):
                    window[part] = jnp.where(first_tile == tile - part, values, window[part])
            for part in range(2):
                at = (2 * side + part) * LANES
                out_ref[rows_of, at : at + LANES] = window[part]
    if streamed:
        feet_copy.wait()


def sound(mine_ref, theirs_ref, feet_ref, other_feet_ref):
    block_count, sound_count, window = feet_ref.shape
    rows = mine_ref.shape[0]
    own = (mine_ref[:, :window] + theirs_ref[:, window:]).astype(jnp.bfloat16)
    other = (mine_ref[:, window:] + theirs_ref[:, :window]).astype(jnp.bfloat16)
    block_index = block_of_row((rows, sound_count), block_count)
    image = jnp.zeros((rows, sound_count), jnp.float32)
    for block in range(block_count):
        part = dot(own, feet_ref[block], ((1,), (1,)))
        part = part + dot(other, other_feet_ref[block], ((1,), (1,)))
        image = jnp.where(block_index == block, part, image)
    return image


def turn_kernel(mine_ref, theirs_ref, feet_ref, other_feet_ref, tile_rows_ref, out_ref, image_ref):
    image = sound(mine_ref, theirs_ref, feet_ref, other_feet_ref)
    image_ref[...] = image
    pieces = adjoint_pieces(image.astype(jnp.bfloat16), feet_ref)
    tile_rows = tile_rows_ref[...]
    size = 2 * feet_ref.shape[0]
    probe_count = image.shape[0] // feet_ref.shape[0]
    count = out_ref.shape[0] // size * 3 // 4
    for pair in range(count):
        tiles = [
            swap_quarters(
                placed_tile(pieces, tile_rows, *divmod(2 * pair + part, probe_count), probe_count)
            )
            for part in range(2)
        ]
        out_ref[size * pair : size * (pair + 1), :] = jnp.concatenate(tiles, axis=0).astype(
            jnp.bfloat16
        )
    out_ref[size * count :, :] = jnp.zeros((out_ref.shape[0] - size * count, LANES), jnp.bfloat16)


def last_kernel(probe_count, mine_ref, theirs_ref, feet_ref, other_feet_ref, probes_ref, first_ref, sums_ref, second_ref):
    second = sound(mine_ref, theirs_ref, feet_ref, other_feet_ref)
    second_ref[...] = second
    probes = probes_ref[...]
    first = first_ref[...]
    block_count = second.shape[0] // probe_count
    lane = lax.broadcasted_iota(jnp.int32, (1, LANES), 1)
    row = jnp.zeros((1, LANES), jnp.float32)
    pairs = (
        (probes, probes),
        (probes, first),
        (first, first),
        (probes, second),
        (first, second),
        (second, second),
    )
    for place, (left, right) in enumerate(pairs):
        product = left * right
        for probe in range(probe_count):
            value = jnp.sum(
                product[probe * block_count : (probe + 1) * block_count], axis=0, keepdims=True
            )
            value = jnp.sum(value, axis=1, keepdims=True)
            row = jnp.where(lane == place * probe_count + probe, value, row)
    sums_ref[...] = jnp.broadcast_to(row, sums_ref.shape)


def finish_kernel(total_rows, sums_ref, probes_ref, first_ref, second_ref, coefficients_ref, residual_ref):
    block_count, probe_count, half_sound = residual_ref.shape
    row = jnp.sum(sums_ref[...], axis=0, keepdims=True) / total_rows

    def stat(place):
        shift = (LANES - place * probe_count) % LANES
        return row if shift == 0 else pltpu.roll(row, shift, 1)

    pp, pw, ww, px, wx, xx = [stat(place) for place in range(6)]
    scale_square = pp + epsilon
    scale = jnp.sqrt(scale_square)
    alpha_one = pw / scale_square
    rest = (ww - 2.0 * alpha_one * pw + alpha_one * alpha_one * pp) / scale_square
    beta_one = jnp.sqrt(jnp.maximum(rest, 0.0) + epsilon)
    cross = wx - alpha_one * ww - alpha_one * px + alpha_one * alpha_one * pw
    alpha_two = (cross / (beta_one * beta_one) - (pw - alpha_one * pp)) / scale_square
    of_second = 1.0 / (scale * beta_one)
    of_first = -(alpha_one + alpha_two) * of_second
    of_probes = (alpha_one * alpha_two / beta_one - beta_one) / scale
    square = (
        of_second * of_second * xx
        + of_first * of_first * ww
        + of_probes * of_probes * pp
        + 2.0 * (of_second * of_first * wx + of_second * of_probes * px + of_first * of_probes * pw)
    )
    beta_two = jnp.sqrt(jnp.maximum(square, 0.0) + epsilon)
    for place, value in enumerate((alpha_one, beta_one, alpha_two, beta_two)):
        coefficients_ref[place : place + 1, :] = value[:, :probe_count]
    at = pl.multiple_of(lax.axis_index("half") * half_sound, LANES)
    for probe in range(probe_count):
        rows = slice(probe * block_count, (probe + 1) * block_count)
        residual_ref[:, probe, :] = (
            of_second[:, probe : probe + 1] * second_ref[rows, pl.ds(at, half_sound)]
            + of_first[:, probe : probe + 1] * first_ref[rows, pl.ds(at, half_sound)]
            + of_probes[:, probe : probe + 1] * probes_ref[rows, pl.ds(at, half_sound)]
        )


def body(probes, footprints, lag_weights, owners, window_tiles, coords, temporal):
    periods = lax.axis_size("period")
    block_count, top_count = owners.shape
    probe_count = probes.shape[1]
    sound_count = footprints.shape[1]
    window = footprints.shape[2]
    cell_count = coords.shape[1]
    half_cells = cell_count // 2
    rows = block_count * probe_count
    total_rows = float(block_count * periods * sound_count)
    f32, bf16 = jnp.float32, jnp.bfloat16
    wire = pltpu.VMEM((periods * HALF_SUBLANES, LANES), bf16)
    vectors = pltpu.VMEM((rows, sound_count), f32)

    def call(kernel, scalars, values, outputs, scratch=(), left_in_hbm=()):
        outputs = tuple(outputs)
        results = pl.pallas_call(
            kernel,
            out_shape=outputs,
            in_specs=[smem] * len(scalars) + [vmem] * len(values) + [hbm] * len(left_in_hbm),
            out_specs=tuple(vmem for _ in outputs),
            scratch_shapes=list(scratch),
            compiler_params=small,
        )(
            *scalars,
            *[in_vmem(value) for value in values],
            *[in_hbm(value) for value in left_in_hbm],
        )
        return results if len(outputs) > 1 else results[0]

    def send(value):
        count = value.shape[0] // periods
        return exchange(value.reshape(periods, count, LANES)).reshape(value.shape)

    depth, width = 256, 512
    block_rows = half_cells // depth

    def first_build():
        return pl.pallas_call(
            first_build_kernel,
            out_shape=(
                pltpu.HBM((half_cells, half_cells), bf16),
                pltpu.HBM((depth, half_cells), bf16),
            ),
            in_specs=[vmem, vmem],
            out_specs=(hbm, hbm),
            scratch_shapes=[
                pltpu.VMEM((block_rows + 1, depth, half_cells), bf16),
                pltpu.SemaphoreType.DMA((block_rows + 1,)),
            ],
            compiler_params=small,
            name="first_build",
        )(in_vmem(left), in_vmem(right))

    def second_build():
        return pl.pallas_call(
            second_build_kernel,
            out_shape=pltpu.HBM((half_cells - depth, half_cells), bf16),
            grid=(block_rows - 1,),
            in_specs=[
                pl.BlockSpec((16, depth), lambda i: (0, i + 1)),
                pl.BlockSpec((16, half_cells), lambda i: (0, 1)),
            ],
            out_specs=pl.BlockSpec((depth, half_cells), lambda i: (i, 0)),
            compiler_params=small,
            name="second_build",
        )(in_vmem(left), in_vmem(right))

    def spatial_step(received, kept):
        scratch = [pltpu.VMEM((rows, half_cells), f32), pltpu.VMEM((rows, cell_count), f32)]
        outputs = [pltpu.VMEM((rows, 2 * window), f32)]
        values, stored = (received, tile_rows, other_rows), ()
        if kept is None:
            outputs.append(pltpu.VMEM((2, half_cells, half_cells), bf16))
            outputs.append(pltpu.VMEM(footprints.shape, bf16))
            count = block_rows + 2 * half_cells // width + 1
            scratch.append(pltpu.SemaphoreType.DMA((count,)))
            stored = (own_spatial, top_spatial, rest_spatial, other_feet)
        else:
            values = values + (kept,)
        results = call(
            functools.partial(spatial_kernel, block_count, depth, width, kept is None),
            (),
            values,
            outputs,
            scratch,
            stored,
        )
        if kept is None:
            mine, kept, feet = results
            return mine, from_other_half(mine), kept, feet
        return results, from_other_half(results)

    tiles = window_tiles.reshape(-1)
    other_probes = from_other_half(probes)
    other_tiles = from_other_half(tiles)
    own_probes, table, tile_rows, left, right, first_feet = call(
        prepare_kernel,
        (),
        (),
        (
            pltpu.VMEM((rows, sound_count // 2), f32),
            pltpu.VMEM((2 * HALF_SUBLANES, LANES), f32),
            pltpu.VMEM((2 * HALF_SUBLANES, LANES), jnp.int32),
            pltpu.VMEM((16, half_cells), bf16),
            pltpu.VMEM((16, cell_count), bf16),
            pltpu.VMEM(footprints.shape, bf16),
        ),
        (
            pltpu.SMEM(tiles.shape, jnp.int32),
            pltpu.SMEM((top_count, block_count), jnp.int32),
            pltpu.SMEM((top_count, block_count), f32),
            pltpu.VMEM(probes.shape, f32),
            pltpu.VMEM(coords.shape, jnp.int32),
            pltpu.SemaphoreType.DMA((6,)),
        ),
        (tiles, owners.T, lag_weights.T, probes, coords, footprints),
    )
    to_mix, all_probes, other_rows = call(
        start_kernel,
        (),
        (own_probes, other_probes, table, tile_rows, first_feet, other_tiles.reshape(1, -1)),
        (wire, vectors, pltpu.VMEM((block_count, LANES), jnp.int32)),
    )
    received = send(to_mix)
    other_feet = from_other_half(footprints)
    own_spatial, top_spatial = first_build()
    received, own_spatial, top_spatial = lax.optimization_barrier(
        (received, own_spatial, top_spatial)
    )
    mixed, choice = call(
        functools.partial(first_mix_kernel, top_count),
        (),
        (received, temporal),
        (wire, pltpu.VMEM((2 * periods, periods * HALF_SUBLANES), bf16)),
    )
    rest_spatial = second_build()
    mine, theirs, kept, other_feet = spatial_step(send(mixed), None)
    to_mix, first = call(
        turn_kernel, (), (mine, theirs, footprints, other_feet, tile_rows), (wire, vectors)
    )
    mixed = call(mix_kernel, (), (send(to_mix), temporal, choice), (wire,))
    mine, theirs = spatial_step(send(mixed), kept)
    sums, second = call(
        functools.partial(last_kernel, probe_count),
        (),
        (mine, theirs, footprints, other_feet, all_probes, first),
        (pltpu.VMEM((periods, LANES), f32), vectors),
    )
    sums = exchange(sums.reshape(periods, 1, LANES)).reshape(periods, LANES)
    return pl.pallas_call(
        functools.partial(finish_kernel, total_rows),
        out_shape=(
            jax.ShapeDtypeStruct((4, probe_count), f32),
            jax.ShapeDtypeStruct(probes.shape, f32),
        ),
        in_specs=[vmem, vmem, vmem, vmem],
        out_specs=(vmem, vmem),
        compiler_params=small,
        name="finish",
    )(in_vmem(sums), in_vmem(all_probes), in_vmem(first), in_vmem(second))


def solution(mesh):
    in_specs = (
        P("period", None, "half"),
        P("period", None, "half"),
        P("period", None),
        P("period", None),
        P("period", "half"),
        P(),
        P(),
    )
    out_specs = (P(), P("period", None, "half"))
    return jax.shard_map(body, mesh=mesh, in_specs=in_specs, out_specs=out_specs, check_vma=False)
```

```python
import functools

import jax
import jax.numpy as jnp
from jax import lax
from jax.experimental import pallas as pl
from jax.experimental.pallas import tpu as pltpu
from jax.sharding import PartitionSpec as P


epsilon = 1e-06
kernel_scale = 0.05
kernel_length = 6.0
log2e = 1.4426950408889634
LANES = 128
HALF_LANES = 64
HALF_SUBLANES = 4
GROUP = 48


smem = pl.BlockSpec(memory_space=pltpu.SMEM)
vmem = pl.BlockSpec(memory_space=pltpu.VMEM)
hbm = pl.BlockSpec(memory_space=pltpu.HBM)
small = pltpu.CompilerParams(vmem_limit_bytes=24 * 1024 * 1024)


def in_hbm(value):
    return pltpu.with_memory_space_constraint(value, pltpu.HBM)


def in_vmem(value):
    return pltpu.with_memory_space_constraint(value, pltpu.VMEM)


def from_other_half(value):
    return lax.ppermute(value, "half", [(0, 1), (1, 0)])


def exchange(value):
    return lax.all_to_all(value, "period", split_axis=0, concat_axis=0, tiled=True)


def block_of_row(shape, block_count):
    return lax.rem(lax.broadcasted_iota(jnp.int32, shape, 0), block_count)


def halves(value):
    high = value.astype(jnp.bfloat16)
    low = (value - high.astype(jnp.float32)).astype(jnp.bfloat16)
    return high, low


def dot(left, right, dims=((1,), (0,))):
    return lax.dot_general(left, right, (dims, ((), ())), preferred_element_type=jnp.float32)


def tile_iotas():
    row = lax.broadcasted_iota(jnp.int32, (2 * HALF_SUBLANES, LANES), 0)
    lane = lax.broadcasted_iota(jnp.int32, (2 * HALF_SUBLANES, LANES), 1)
    return row, lane


def half_turn(tile):
    return pltpu.roll(tile, HALF_SUBLANES, 0)


def swap_quarters(tile):
    row, lane = tile_iotas()
    turned = half_turn(pltpu.roll(tile, HALF_LANES, 1))
    return jnp.where((row < HALF_SUBLANES) == (lane < HALF_LANES), tile, turned)


def group_span(group):
    return divmod(GROUP * group, LANES)


def pack_groups(tiles):
    row, lane = tile_iotas()
    left = lane < HALF_LANES
    diagonal = (row < HALF_SUBLANES) == left
    packed = []
    for pair in range(4):
        first, second = [], []
        for group in (2 * pair, 2 * pair + 1):
            place, at = group_span(group)
            source = tiles[place]
            if at + GROUP > LANES:
                source = jnp.where(lane >= at, source, tiles[place + 1])
            for target, end in ((first, 0), (second, HALF_LANES)):
                shift = (end - at) % LANES
                target.append(pltpu.roll(source, shift, 1) if shift else source)
        kept = jnp.where(left, first[0], second[1])
        moved = half_turn(jnp.where(left, first[1], second[0]))
        packed.append(jnp.where(diagonal, kept, moved))
    return packed


def unpack_groups(packed):
    row, lane = tile_iotas()
    upper = row < HALF_SUBLANES
    groups = []
    for tile in packed:
        turned = pltpu.roll(tile, HALF_LANES, 1)
        groups.append(jnp.where(upper, tile, half_turn(turned)))
        groups.append(jnp.where(upper, half_turn(tile), turned))
    tiles = [None, None, None]
    for group, value in enumerate(groups):
        place, at = group_span(group)
        value = pltpu.roll(value, at, 1) if at else value
        tiles[place] = value if at == 0 else jnp.where(lane >= at, value, tiles[place])
        if at + GROUP > LANES:
            tiles[place + 1] = value
    return tiles


def adjoint_pieces(vector, feet_ref):
    block_count, _, window = feet_ref.shape
    block_index = block_of_row((vector.shape[0], window), block_count)
    pieces = jnp.zeros((vector.shape[0], window), jnp.float32)
    for block in range(block_count):
        pieces = jnp.where(block_index == block, dot(vector, feet_ref[block]), pieces)
    return pieces


def placed_tile(pieces, tile_rows, tile, probe, probe_count):
    count = pieces.shape[0] // probe_count
    rows = slice(probe * count, (probe + 1) * count)
    value = jnp.where(tile_rows == tile, pieces[rows, :LANES], 0.0)
    return jnp.where(tile_rows == tile - 1, pieces[rows, LANES:], value)


def distance_terms(cells, turned):
    x, y = cells[0:1], cells[1:2]
    norm = x * x + y * y
    low = (norm & 255).astype(jnp.float32)
    high = (norm - (norm & 255)).astype(jnp.float32)
    x, y, one = x.astype(jnp.float32), y.astype(jnp.float32), jnp.ones(x.shape, jnp.float32)
    if turned:
        terms = [-2.0 * x, -2.0 * y, one, one, high, low]
    else:
        terms = [x, y, high, low, one, one]
    row = lax.broadcasted_iota(jnp.int32, (16, x.shape[1]), 0)
    result = jnp.zeros((16, x.shape[1]), jnp.float32)
    for place, term in enumerate(terms):
        result = jnp.where(row == place, term, result)
    return result.astype(jnp.bfloat16)


def prepare_kernel(tiles_in, owners_in, weights_in, own_in, coords_in, feet_in, own_ref, table_ref, tile_rows_ref, left_ref, right_ref, feet_ref, tiles_ref, owners_ref, weights_ref, probes_ref, coords_ref, sems):
    block_count, probe_count, _ = probes_ref.shape
    top_count = owners_ref.shape[0]
    pairs = (
        (tiles_in, tiles_ref),
        (owners_in, owners_ref),
        (weights_in, weights_ref),
        (own_in, probes_ref),
        (coords_in, coords_ref),
        (feet_in, feet_ref),
    )
    copies = [
        pltpu.make_async_copy(source, target, sems.at[place])
        for place, (source, target) in enumerate(pairs)
    ]
    for copy in copies:
        copy.start()
    for copy in copies[:5]:
        copy.wait()
    for probe in range(probe_count):
        rows = slice(probe * block_count, (probe + 1) * block_count)
        own_ref[rows, :] = probes_ref[:, probe, :]
    row, lane = tile_iotas()
    owner = jnp.zeros(row.shape, jnp.float32)
    weight = jnp.zeros(row.shape, jnp.float32)
    for block in range(block_count):
        column, turn = divmod(block, HALF_SUBLANES)
        for top in range(top_count):
            here = lane == column * HALF_LANES + GROUP + top
            here = here & (lax.rem(row, HALF_SUBLANES) == turn)
            owner = jnp.where(here, owners_ref[top, block].astype(jnp.float32), owner)
            weight = jnp.where(here, weights_ref[top, block], weight)
    table_ref[...] = owner + pltpu.roll(weight, top_count, 1)
    tile_rows = jnp.zeros(row.shape, jnp.int32)
    for block in range(block_count):
        tile_rows = jnp.where(row == block, tiles_ref[block], tile_rows)
    tile_rows_ref[...] = tile_rows
    half = lax.axis_index("half")
    half_cells = left_ref.shape[1]
    own_at = pl.multiple_of(half * half_cells, LANES)
    other_at = pl.multiple_of((1 - half) * half_cells, LANES)
    own = coords_ref[:, pl.ds(own_at, half_cells)]
    left_ref[...] = distance_terms(own, False)
    right_ref[:, :half_cells] = distance_terms(own, True)
    right_ref[:, half_cells:] = distance_terms(coords_ref[:, pl.ds(other_at, half_cells)], True)
    copies[5].wait()


def start_kernel(own_ref, other_ref, table_ref, tile_rows_ref, feet_ref, out_ref, probes_ref):
    half = lax.axis_index("half")
    block_count, probe_count, half_sound = other_ref.shape
    own_at = pl.multiple_of(half * half_sound, LANES)
    other_at = pl.multiple_of((1 - half) * half_sound, LANES)
    probes_ref[:, pl.ds(own_at, half_sound)] = own_ref[...]
    for probe in range(probe_count):
        rows = slice(probe * block_count, (probe + 1) * block_count)
        probes_ref[rows, pl.ds(other_at, half_sound)] = other_ref[:, probe, :]
    pieces = adjoint_pieces(probes_ref[...].astype(jnp.bfloat16), feet_ref)
    table, tile_rows = table_ref[...], tile_rows_ref[...]
    _, lane = tile_iotas()
    data = lax.rem(lane, HALF_LANES) < GROUP
    size = 2 * block_count
    triples = out_ref.shape[0] // (2 * size * probe_count)
    for probe in range(probe_count):
        for triple in range(triples):
            packed = pack_groups(
                [
                    placed_tile(pieces, tile_rows, 3 * triple + part, probe, probe_count)
                    for part in range(3)
                ]
            )
            packed = [jnp.where(data, tile, table) for tile in packed]
            at = 2 * size * (probe * triples + triple)
            for part in range(2):
                out_ref[at + part * size : at + (part + 1) * size, :] = jnp.concatenate(
                    packed[2 * part : 2 * part + 2], axis=0
                ).astype(jnp.bfloat16)


def spatial_values(left, right):
    squared = jnp.maximum(dot(left, right, ((0,), (0,))), 1e-12)
    distance = squared * lax.rsqrt(squared)
    return jnp.exp2(distance * (-log2e / kernel_length)).astype(jnp.bfloat16)


def first_build_kernel(left_ref, right_ref, own_out, top_out, buffers, sems):
    half_cells = left_ref.shape[1]
    depth = buffers.shape[1]
    count = half_cells // depth
    copies = []
    for place in range(count + 1):
        at = depth * (place % count)
        if place < count:
            right = right_ref[:, at:half_cells]
            target = own_out.at[at : at + depth, at:]
        else:
            right = right_ref[:, half_cells:]
            target = top_out
        buffers[place, :, at:] = spatial_values(left_ref[:, at : at + depth], right)
        copy = pltpu.make_async_copy(buffers.at[place, :, at:], target, sems.at[place])
        copy.start()
        copies.append(copy)
    for copy in copies:
        copy.wait()


def second_build_kernel(left_ref, right_ref, out, buffers, sems):
    half_cells = left_ref.shape[1]
    count, depth = buffers.shape[:2]
    copies = []
    for place in range(count):
        at = depth * (place + 1)
        buffers[place] = spatial_values(
            left_ref[:, at : at + depth], right_ref[:, half_cells:]
        )
        copies.append(
            pltpu.make_async_copy(
                buffers.at[place], out.at[at - depth : at], sems.at[place]
            )
        )
        copies[-1].start()
    for copy in copies:
        copy.wait()


def mix(received, choice, temporal):
    periods = temporal.shape[0]
    both = dot(choice, received)
    gathered = both[:periods] + pltpu.roll(both[periods:], HALF_LANES, 1)
    high, low = halves(gathered * kernel_scale)
    temporal_high, temporal_low = halves(temporal)
    turned = ((0,), (1,))
    mixed = dot(high, temporal_high, turned) + dot(high, temporal_low, turned)
    mixed = (mixed + dot(low, temporal_high, turned))[:HALF_LANES].astype(jnp.bfloat16)
    nothing = jnp.zeros(mixed.shape, jnp.bfloat16)
    upper = jnp.concatenate([mixed, nothing], axis=1)
    lower = jnp.concatenate([nothing, mixed], axis=1)
    return dot(jnp.concatenate([upper, lower], axis=0), choice).T.astype(jnp.bfloat16)


def first_mix_kernel(top_count, received_ref, temporal_ref, others_ref, out_ref, choice_ref, other_rows_ref):
    block_count = others_ref.shape[1]
    square = (block_count, block_count)
    on_diagonal = lax.broadcasted_iota(jnp.int32, square, 0) == lax.broadcasted_iota(
        jnp.int32, square, 1
    )
    others = jnp.where(on_diagonal, jnp.broadcast_to(others_ref[...], square), 0)
    others = jnp.sum(others, axis=1, keepdims=True)
    other_rows_ref[...] = jnp.broadcast_to(others, other_rows_ref.shape)
    periods = temporal_ref.shape[0]
    wide = received_ref[...].astype(jnp.float32).T
    shape = (periods, wide.shape[1])
    period = lax.broadcasted_iota(jnp.int32, shape, 0).astype(jnp.float32)
    for column in range(2):
        choice = jnp.zeros(shape, jnp.float32)
        for top in range(top_count):
            at = column * HALF_LANES + GROUP + top
            weight = wide[at + top_count : at + top_count + 1]
            choice = jnp.where(wide[at : at + 1] == period, weight, choice)
        choice_ref[column * periods : (column + 1) * periods, :] = choice.astype(jnp.bfloat16)
    out_ref[...] = mix(received_ref[...], choice_ref[...], temporal_ref[...])


def mix_kernel(received_ref, temporal_ref, choice_ref, out_ref):
    out_ref[...] = mix(received_ref[...], choice_ref[...], temporal_ref[...])


def spatial_kernel(block_count, depth, width, streamed, received_ref, tile_rows_ref, other_rows_ref, *refs):
    if streamed:
        own_in, top_in, rest_in, feet_in, out_ref, kept_ref, feet_ref, field, total, sems = refs
    else:
        kept_ref, out_ref, field, total = refs
    rows, half_cells = field.shape
    probe_count = rows // block_count
    tile_count = half_cells // LANES
    own_copies, other_copies = [], []
    if streamed:
        pairs = [
            (own_in.at[at : at + depth, at:], kept_ref.at[0, at : at + depth, at:])
            for at in range(0, half_cells, depth)
        ]
        for at in range(0, half_cells, width):
            columns = slice(at, at + width)
            pairs.append((top_in.at[:, columns], kept_ref.at[1, :depth, columns]))
            pairs.append((rest_in.at[:, columns], kept_ref.at[1, depth:, columns]))
        pairs.append((feet_in, feet_ref))
        copies = [
            pltpu.make_async_copy(source, target, sems.at[place])
            for place, (source, target) in enumerate(pairs)
        ]
        for copy in copies:
            copy.start()
        own_copies, other_copies = copies[: half_cells // depth], copies[half_cells // depth :]
        feet_copy = copies[-1]
    size = 2 * block_count

    def unpack(probe, carry):
        into = pl.multiple_of(probe * block_count, block_count)
        for triple in range(tile_count // 3):
            at = pl.multiple_of(2 * size * (probe * (tile_count // 3) + triple), size)
            both = received_ref[pl.ds(at, 2 * size), :].astype(jnp.float32)
            packed = [both[part * block_count : (part + 1) * block_count] for part in range(4)]
            for part, value in enumerate(unpack_groups(packed)):
                start = (3 * triple + part) * LANES
                field[pl.ds(into, block_count), start : start + LANES] = value
        return carry

    if streamed:
        lax.fori_loop(0, probe_count, unpack, 0)
    else:
        for pair in range(tile_count * probe_count // 2):
            both = received_ref[size * pair : size * (pair + 1), :].astype(jnp.float32)
            for part in range(2):
                tile, probe = divmod(2 * pair + part, probe_count)
                field[
                    probe * block_count : (probe + 1) * block_count,
                    tile * LANES : (tile + 1) * LANES,
                ] = swap_quarters(both[part * block_count : (part + 1) * block_count])
    cells = field[...].astype(jnp.bfloat16)
    for copy in own_copies:
        copy.wait()
    for at in range(0, half_cells, depth):
        end = at + depth
        value = dot(cells[:, :end], kept_ref[0, :end, at:end])
        if end < half_cells:
            value = value + dot(cells[:, end:], kept_ref[0, at:end, end:], ((1,), (1,)))
        total[:, at:end] = value
    for place, at in enumerate(range(0, half_cells, width)):
        for copy in other_copies[2 * place : 2 * place + 2]:
            copy.wait()
        start = half_cells + at
        total[:, start : start + width] = dot(cells, kept_ref[1, :, at : at + width])
    nothing = jnp.zeros((block_count, LANES), jnp.float32)
    for side, rows_ref in enumerate((tile_rows_ref, other_rows_ref)):
        first_tile = rows_ref[...]
        for probe in range(probe_count):
            rows_of = slice(probe * block_count, (probe + 1) * block_count)
            window = [nothing, nothing]
            for tile in range(tile_count):
                at = side * half_cells + tile * LANES
                values = total[rows_of, at : at + LANES]
                for part in range(2):
                    window[part] = jnp.where(first_tile == tile - part, values, window[part])
            for part in range(2):
                at = (2 * side + part) * LANES
                out_ref[rows_of, at : at + LANES] = window[part]
    if streamed:
        feet_copy.wait()


def sound(mine_ref, theirs_ref, feet_ref, other_feet_ref):
    block_count, sound_count, window = feet_ref.shape
    rows = mine_ref.shape[0]
    own = (mine_ref[:, :window] + theirs_ref[:, window:]).astype(jnp.bfloat16)
    other = (mine_ref[:, window:] + theirs_ref[:, :window]).astype(jnp.bfloat16)
    block_index = block_of_row((rows, sound_count), block_count)
    image = jnp.zeros((rows, sound_count), jnp.float32)
    for block in range(block_count):
        part = dot(own, feet_ref[block], ((1,), (1,)))
        part = part + dot(other, other_feet_ref[block], ((1,), (1,)))
        image = jnp.where(block_index == block, part, image)
    return image


def turn_kernel(mine_ref, theirs_ref, feet_ref, other_feet_ref, tile_rows_ref, out_ref, image_ref):
    image = sound(mine_ref, theirs_ref, feet_ref, other_feet_ref)
    image_ref[...] = image
    pieces = adjoint_pieces(image.astype(jnp.bfloat16), feet_ref)
    tile_rows = tile_rows_ref[...]
    size = 2 * feet_ref.shape[0]
    probe_count = image.shape[0] // feet_ref.shape[0]
    count = out_ref.shape[0] // size * 3 // 4
    for pair in range(count):
        tiles = [
            swap_quarters(
                placed_tile(pieces, tile_rows, *divmod(2 * pair + part, probe_count), probe_count)
            )
            for part in range(2)
        ]
        out_ref[size * pair : size * (pair + 1), :] = jnp.concatenate(tiles, axis=0).astype(
            jnp.bfloat16
        )
    out_ref[size * count :, :] = jnp.zeros((out_ref.shape[0] - size * count, LANES), jnp.bfloat16)


def last_kernel(probe_count, mine_ref, theirs_ref, feet_ref, other_feet_ref, probes_ref, first_ref, sums_ref, second_ref):
    second = sound(mine_ref, theirs_ref, feet_ref, other_feet_ref)
    second_ref[...] = second
    probes = probes_ref[...]
    first = first_ref[...]
    block_count = second.shape[0] // probe_count
    lane = lax.broadcasted_iota(jnp.int32, (1, LANES), 1)
    row = jnp.zeros((1, LANES), jnp.float32)
    pairs = (
        (probes, probes),
        (probes, first),
        (first, first),
        (probes, second),
        (first, second),
        (second, second),
    )
    for place, (left, right) in enumerate(pairs):
        product = left * right
        for probe in range(probe_count):
            value = jnp.sum(
                product[probe * block_count : (probe + 1) * block_count], axis=0, keepdims=True
            )
            value = jnp.sum(value, axis=1, keepdims=True)
            row = jnp.where(lane == place * probe_count + probe, value, row)
    sums_ref[...] = jnp.broadcast_to(row, sums_ref.shape)


def finish_kernel(total_rows, sums_ref, probes_ref, first_ref, second_ref, coefficients_ref, residual_ref):
    block_count, probe_count, half_sound = residual_ref.shape
    row = jnp.sum(sums_ref[...], axis=0, keepdims=True) / total_rows

    def stat(place):
        shift = (LANES - place * probe_count) % LANES
        return row if shift == 0 else pltpu.roll(row, shift, 1)

    pp, pw, ww, px, wx, xx = [stat(place) for place in range(6)]
    scale_square = pp + epsilon
    scale = jnp.sqrt(scale_square)
    alpha_one = pw / scale_square
    rest = (ww - 2.0 * alpha_one * pw + alpha_one * alpha_one * pp) / scale_square
    beta_one = jnp.sqrt(jnp.maximum(rest, 0.0) + epsilon)
    cross = wx - alpha_one * ww - alpha_one * px + alpha_one * alpha_one * pw
    alpha_two = (cross / (beta_one * beta_one) - (pw - alpha_one * pp)) / scale_square
    of_second = 1.0 / (scale * beta_one)
    of_first = -(alpha_one + alpha_two) * of_second
    of_probes = (alpha_one * alpha_two / beta_one - beta_one) / scale
    square = (
        of_second * of_second * xx
        + of_first * of_first * ww
        + of_probes * of_probes * pp
        + 2.0 * (of_second * of_first * wx + of_second * of_probes * px + of_first * of_probes * pw)
    )
    beta_two = jnp.sqrt(jnp.maximum(square, 0.0) + epsilon)
    for place, value in enumerate((alpha_one, beta_one, alpha_two, beta_two)):
        coefficients_ref[place : place + 1, :] = value[:, :probe_count]
    at = pl.multiple_of(lax.axis_index("half") * half_sound, LANES)
    for probe in range(probe_count):
        rows = slice(probe * block_count, (probe + 1) * block_count)
        residual_ref[:, probe, :] = (
            of_second[:, probe : probe + 1] * second_ref[rows, pl.ds(at, half_sound)]
            + of_first[:, probe : probe + 1] * first_ref[rows, pl.ds(at, half_sound)]
            + of_probes[:, probe : probe + 1] * probes_ref[rows, pl.ds(at, half_sound)]
        )


def body(probes, footprints, lag_weights, owners, window_tiles, coords, temporal):
    periods = lax.axis_size("period")
    block_count, top_count = owners.shape
    probe_count = probes.shape[1]
    sound_count = footprints.shape[1]
    window = footprints.shape[2]
    cell_count = coords.shape[1]
    half_cells = cell_count // 2
    rows = block_count * probe_count
    total_rows = float(block_count * periods * sound_count)
    f32, bf16 = jnp.float32, jnp.bfloat16
    wire = pltpu.VMEM((periods * HALF_SUBLANES, LANES), bf16)
    vectors = pltpu.VMEM((rows, sound_count), f32)

    def call(kernel, scalars, values, outputs, scratch=(), left_in_hbm=()):
        outputs = tuple(outputs)
        results = pl.pallas_call(
            kernel,
            out_shape=outputs,
            in_specs=[smem] * len(scalars) + [vmem] * len(values) + [hbm] * len(left_in_hbm),
            out_specs=tuple(vmem for _ in outputs),
            scratch_shapes=list(scratch),
            compiler_params=small,
        )(
            *scalars,
            *[in_vmem(value) for value in values],
            *[in_hbm(value) for value in left_in_hbm],
        )
        return results if len(outputs) > 1 else results[0]

    def send(value):
        count = value.shape[0] // periods
        return exchange(value.reshape(periods, count, LANES)).reshape(value.shape)

    depth, width = 256, 512
    block_rows = half_cells // depth

    def first_build():
        return pl.pallas_call(
            first_build_kernel,
            out_shape=(
                pltpu.HBM((half_cells, half_cells), bf16),
                pltpu.HBM((depth, half_cells), bf16),
            ),
            in_specs=[vmem, vmem],
            out_specs=(hbm, hbm),
            scratch_shapes=[
                pltpu.VMEM((block_rows + 1, depth, half_cells), bf16),
                pltpu.SemaphoreType.DMA((block_rows + 1,)),
            ],
            compiler_params=small,
            name="first_build",
        )(in_vmem(left), in_vmem(right))

    def second_build():
        return pl.pallas_call(
            second_build_kernel,
            out_shape=pltpu.HBM((half_cells - depth, half_cells), bf16),
            in_specs=[vmem, vmem],
            out_specs=hbm,
            scratch_shapes=[
                pltpu.VMEM((block_rows - 1, depth, half_cells), bf16),
                pltpu.SemaphoreType.DMA((block_rows - 1,)),
            ],
            compiler_params=small,
            name="second_build",
        )(in_vmem(left), in_vmem(right))

    def spatial_step(received, kept):
        scratch = [pltpu.VMEM((rows, half_cells), f32), pltpu.VMEM((rows, cell_count), f32)]
        outputs = [pltpu.VMEM((rows, 2 * window), f32)]
        values, stored = (received, tile_rows, other_rows), ()
        if kept is None:
            outputs.append(pltpu.VMEM((2, half_cells, half_cells), bf16))
            outputs.append(pltpu.VMEM(footprints.shape, bf16))
            count = block_rows + 2 * half_cells // width + 1
            scratch.append(pltpu.SemaphoreType.DMA((count,)))
            stored = (own_spatial, top_spatial, rest_spatial, other_feet)
        else:
            values = values + (kept,)
        results = call(
            functools.partial(spatial_kernel, block_count, depth, width, kept is None),
            (),
            values,
            outputs,
            scratch,
            stored,
        )
        if kept is None:
            mine, kept, feet = results
            return mine, from_other_half(mine), kept, feet
        return results, from_other_half(results)

    tiles = window_tiles.reshape(-1)
    other_probes = from_other_half(probes)
    own_probes, table, tile_rows, left, right, first_feet = call(
        prepare_kernel,
        (),
        (),
        (
            pltpu.VMEM((rows, sound_count // 2), f32),
            pltpu.VMEM((2 * HALF_SUBLANES, LANES), f32),
            pltpu.VMEM((2 * HALF_SUBLANES, LANES), jnp.int32),
            pltpu.VMEM((16, half_cells), bf16),
            pltpu.VMEM((16, cell_count), bf16),
            pltpu.VMEM(footprints.shape, bf16),
        ),
        (
            pltpu.SMEM(tiles.shape, jnp.int32),
            pltpu.SMEM((top_count, block_count), jnp.int32),
            pltpu.SMEM((top_count, block_count), f32),
            pltpu.VMEM(probes.shape, f32),
            pltpu.VMEM(coords.shape, jnp.int32),
            pltpu.SemaphoreType.DMA((6,)),
        ),
        (tiles, owners.T, lag_weights.T, probes, coords, footprints),
    )
    to_mix, all_probes = call(
        start_kernel, (), (own_probes, other_probes, table, tile_rows, first_feet), (wire, vectors)
    )
    received = send(to_mix)
    other_feet = from_other_half(footprints)
    other_tiles = from_other_half(tiles)
    own_spatial, top_spatial = first_build()
    received, own_spatial, top_spatial = lax.optimization_barrier(
        (received, own_spatial, top_spatial)
    )
    mixed, choice, other_rows = call(
        functools.partial(first_mix_kernel, top_count),
        (),
        (received, temporal, other_tiles.reshape(1, -1)),
        (
            wire,
            pltpu.VMEM((2 * periods, periods * HALF_SUBLANES), bf16),
            pltpu.VMEM((block_count, LANES), jnp.int32),
        ),
    )
    rest_spatial = second_build()
    mine, theirs, kept, other_feet = spatial_step(send(mixed), None)
    to_mix, first = call(
        turn_kernel, (), (mine, theirs, footprints, other_feet, tile_rows), (wire, vectors)
    )
    mixed = call(mix_kernel, (), (send(to_mix), temporal, choice), (wire,))
    mine, theirs = spatial_step(send(mixed), kept)
    sums, second = call(
        functools.partial(last_kernel, probe_count),
        (),
        (mine, theirs, footprints, other_feet, all_probes, first),
        (pltpu.VMEM((periods, LANES), f32), vectors),
    )
    sums = exchange(sums.reshape(periods, 1, LANES)).reshape(periods, LANES)
    return pl.pallas_call(
        functools.partial(finish_kernel, total_rows),
        out_shape=(
            jax.ShapeDtypeStruct((4, probe_count), f32),
            jax.ShapeDtypeStruct(probes.shape, f32),
        ),
        in_specs=[vmem, vmem, vmem, vmem],
        out_specs=(vmem, vmem),
        compiler_params=small,
        name="finish",
    )(in_vmem(sums), in_vmem(all_probes), in_vmem(first), in_vmem(second))


def solution(mesh):
    in_specs = (
        P("period", None, "half"),
        P("period", None, "half"),
        P("period", None),
        P("period", None),
        P("period", "half"),
        P(),
        P(),
    )
    out_specs = (P(), P("period", None, "half"))
    return jax.shard_map(body, mesh=mesh, in_specs=in_specs, out_specs=out_specs, check_vma=False)
```

```python
import functools

import jax
import jax.numpy as jnp
from jax import lax
from jax.experimental import pallas as pl
from jax.experimental.pallas import tpu as pltpu
from jax.sharding import PartitionSpec as P


epsilon = 1e-06
kernel_scale = 0.05
kernel_length = 6.0
log2e = 1.4426950408889634
LANES = 128
HALF_LANES = 64
HALF_SUBLANES = 4
GROUP = 48


smem = pl.BlockSpec(memory_space=pltpu.SMEM)
vmem = pl.BlockSpec(memory_space=pltpu.VMEM)
hbm = pl.BlockSpec(memory_space=pltpu.HBM)
small = pltpu.CompilerParams(vmem_limit_bytes=24 * 1024 * 1024)


def in_hbm(value):
    return pltpu.with_memory_space_constraint(value, pltpu.HBM)


def in_vmem(value):
    return pltpu.with_memory_space_constraint(value, pltpu.VMEM)


def from_other_half(value):
    return lax.ppermute(value, "half", [(0, 1), (1, 0)])


def exchange(value):
    return lax.all_to_all(value, "period", split_axis=0, concat_axis=0, tiled=True)


def block_of_row(shape, block_count):
    return lax.rem(lax.broadcasted_iota(jnp.int32, shape, 0), block_count)


def halves(value):
    high = value.astype(jnp.bfloat16)
    low = (value - high.astype(jnp.float32)).astype(jnp.bfloat16)
    return high, low


def dot(left, right, dims=((1,), (0,))):
    return lax.dot_general(left, right, (dims, ((), ())), preferred_element_type=jnp.float32)


def tile_iotas():
    row = lax.broadcasted_iota(jnp.int32, (2 * HALF_SUBLANES, LANES), 0)
    lane = lax.broadcasted_iota(jnp.int32, (2 * HALF_SUBLANES, LANES), 1)
    return row, lane


def half_turn(tile):
    return pltpu.roll(tile, HALF_SUBLANES, 0)


def swap_quarters(tile):
    row, lane = tile_iotas()
    turned = half_turn(pltpu.roll(tile, HALF_LANES, 1))
    return jnp.where((row < HALF_SUBLANES) == (lane < HALF_LANES), tile, turned)


def group_span(group):
    return divmod(GROUP * group, LANES)


def pack_groups(tiles):
    row, lane = tile_iotas()
    left = lane < HALF_LANES
    diagonal = (row < HALF_SUBLANES) == left
    packed = []
    for pair in range(4):
        first, second = [], []
        for group in (2 * pair, 2 * pair + 1):
            place, at = group_span(group)
            source = tiles[place]
            if at + GROUP > LANES:
                source = jnp.where(lane >= at, source, tiles[place + 1])
            for target, end in ((first, 0), (second, HALF_LANES)):
                shift = (end - at) % LANES
                target.append(pltpu.roll(source, shift, 1) if shift else source)
        kept = jnp.where(left, first[0], second[1])
        moved = half_turn(jnp.where(left, first[1], second[0]))
        packed.append(jnp.where(diagonal, kept, moved))
    return packed


def unpack_groups(packed):
    row, lane = tile_iotas()
    upper = row < HALF_SUBLANES
    groups = []
    for tile in packed:
        turned = pltpu.roll(tile, HALF_LANES, 1)
        groups.append(jnp.where(upper, tile, half_turn(turned)))
        groups.append(jnp.where(upper, half_turn(tile), turned))
    tiles = [None, None, None]
    for group, value in enumerate(groups):
        place, at = group_span(group)
        value = pltpu.roll(value, at, 1) if at else value
        tiles[place] = value if at == 0 else jnp.where(lane >= at, value, tiles[place])
        if at + GROUP > LANES:
            tiles[place + 1] = value
    return tiles


def adjoint_pieces(vector, feet_ref):
    block_count, _, window = feet_ref.shape
    block_index = block_of_row((vector.shape[0], window), block_count)
    pieces = jnp.zeros((vector.shape[0], window), jnp.float32)
    for block in range(block_count):
        pieces = jnp.where(block_index == block, dot(vector, feet_ref[block]), pieces)
    return pieces


def placed_tile(pieces, tile_rows, tile, probe, probe_count):
    count = pieces.shape[0] // probe_count
    rows = slice(probe * count, (probe + 1) * count)
    value = jnp.where(tile_rows == tile, pieces[rows, :LANES], 0.0)
    return jnp.where(tile_rows == tile - 1, pieces[rows, LANES:], value)


def distance_terms(cells, turned):
    x, y = cells[0:1], cells[1:2]
    norm = x * x + y * y
    low = (norm & 255).astype(jnp.float32)
    high = (norm - (norm & 255)).astype(jnp.float32)
    x, y, one = x.astype(jnp.float32), y.astype(jnp.float32), jnp.ones(x.shape, jnp.float32)
    if turned:
        terms = [-2.0 * x, -2.0 * y, one, one, high, low]
    else:
        terms = [x, y, high, low, one, one]
    row = lax.broadcasted_iota(jnp.int32, (16, x.shape[1]), 0)
    result = jnp.zeros((16, x.shape[1]), jnp.float32)
    for place, term in enumerate(terms):
        result = jnp.where(row == place, term, result)
    return result.astype(jnp.bfloat16)


def prepare_kernel(tiles_in, owners_in, weights_in, own_in, coords_in, feet_in, own_ref, table_ref, tile_rows_ref, left_ref, right_ref, feet_ref, tiles_ref, owners_ref, weights_ref, probes_ref, coords_ref, sems):
    block_count, probe_count, _ = probes_ref.shape
    top_count = owners_ref.shape[0]
    pairs = (
        (tiles_in, tiles_ref),
        (owners_in, owners_ref),
        (weights_in, weights_ref),
        (own_in, probes_ref),
        (coords_in, coords_ref),
        (feet_in, feet_ref),
    )
    copies = [
        pltpu.make_async_copy(source, target, sems.at[place])
        for place, (source, target) in enumerate(pairs)
    ]
    for copy in copies:
        copy.start()
    for copy in copies[:5]:
        copy.wait()
    for probe in range(probe_count):
        rows = slice(probe * block_count, (probe + 1) * block_count)
        own_ref[rows, :] = probes_ref[:, probe, :]
    row, lane = tile_iotas()
    owner = jnp.zeros(row.shape, jnp.float32)
    weight = jnp.zeros(row.shape, jnp.float32)
    for block in range(block_count):
        column, turn = divmod(block, HALF_SUBLANES)
        for top in range(top_count):
            here = lane == column * HALF_LANES + GROUP + top
            here = here & (lax.rem(row, HALF_SUBLANES) == turn)
            owner = jnp.where(here, owners_ref[top, block].astype(jnp.float32), owner)
            weight = jnp.where(here, weights_ref[top, block], weight)
    table_ref[...] = owner + pltpu.roll(weight, top_count, 1)
    tile_rows = jnp.zeros(row.shape, jnp.int32)
    for block in range(block_count):
        tile_rows = jnp.where(row == block, tiles_ref[block], tile_rows)
    tile_rows_ref[...] = tile_rows
    half = lax.axis_index("half")
    half_cells = left_ref.shape[1]
    own_at = pl.multiple_of(half * half_cells, LANES)
    other_at = pl.multiple_of((1 - half) * half_cells, LANES)
    own = coords_ref[:, pl.ds(own_at, half_cells)]
    left_ref[...] = distance_terms(own, False)
    right_ref[:, :half_cells] = distance_terms(own, True)
    right_ref[:, half_cells:] = distance_terms(coords_ref[:, pl.ds(other_at, half_cells)], True)
    copies[5].wait()


def start_kernel(own_ref, other_ref, table_ref, tile_rows_ref, feet_ref, out_ref, probes_ref):
    half = lax.axis_index("half")
    block_count, probe_count, half_sound = other_ref.shape
    own_at = pl.multiple_of(half * half_sound, LANES)
    other_at = pl.multiple_of((1 - half) * half_sound, LANES)
    probes_ref[:, pl.ds(own_at, half_sound)] = own_ref[...]
    for probe in range(probe_count):
        rows = slice(probe * block_count, (probe + 1) * block_count)
        probes_ref[rows, pl.ds(other_at, half_sound)] = other_ref[:, probe, :]
    pieces = adjoint_pieces(probes_ref[...].astype(jnp.bfloat16), feet_ref)
    table, tile_rows = table_ref[...], tile_rows_ref[...]
    _, lane = tile_iotas()
    data = lax.rem(lane, HALF_LANES) < GROUP
    size = 2 * block_count
    triples = out_ref.shape[0] // (2 * size * probe_count)
    for probe in range(probe_count):
        for triple in range(triples):
            packed = pack_groups(
                [
                    placed_tile(pieces, tile_rows, 3 * triple + part, probe, probe_count)
                    for part in range(3)
                ]
            )
            packed = [jnp.where(data, tile, table) for tile in packed]
            at = 2 * size * (probe * triples + triple)
            for part in range(2):
                out_ref[at + part * size : at + (part + 1) * size, :] = jnp.concatenate(
                    packed[2 * part : 2 * part + 2], axis=0
                ).astype(jnp.bfloat16)


def spatial_values(left, right):
    squared = jnp.maximum(dot(left, right, ((0,), (0,))), 1e-12)
    distance = squared * lax.rsqrt(squared)
    return jnp.exp2(distance * (-log2e / kernel_length)).astype(jnp.bfloat16)


def first_build_kernel(left_ref, right_ref, own_out, top_out, buffers, sems):
    half_cells = left_ref.shape[1]
    depth = buffers.shape[1]
    count = half_cells // depth
    copies = []
    for place in range(count + 1):
        at = depth * (place % count)
        if place < count:
            right = right_ref[:, at:half_cells]
            target = own_out.at[at : at + depth, at:]
        else:
            right = right_ref[:, half_cells:]
            target = top_out
        buffers[place, :, at:] = spatial_values(left_ref[:, at : at + depth], right)
        copy = pltpu.make_async_copy(buffers.at[place, :, at:], target, sems.at[place])
        copy.start()
        copies.append(copy)
    for copy in copies:
        copy.wait()


def second_build_kernel(left_ref, right_ref, out, buffers, sems):
    half_cells = left_ref.shape[1]
    count, depth = buffers.shape[:2]
    copies = []
    for place in range(count):
        at = depth * (place + 1)
        buffers[place] = spatial_values(
            left_ref[:, at : at + depth], right_ref[:, half_cells:]
        )
        copies.append(
            pltpu.make_async_copy(
                buffers.at[place], out.at[at - depth : at], sems.at[place]
            )
        )
        copies[-1].start()
    for copy in copies:
        copy.wait()


def mix(received, choice, temporal):
    periods = temporal.shape[0]
    both = dot(choice, received)
    gathered = both[:periods] + pltpu.roll(both[periods:], HALF_LANES, 1)
    high, low = halves(gathered * kernel_scale)
    temporal_high, temporal_low = halves(temporal)
    turned = ((0,), (1,))
    mixed = dot(high, temporal_high, turned) + dot(high, temporal_low, turned)
    mixed = (mixed + dot(low, temporal_high, turned))[:HALF_LANES].astype(jnp.bfloat16)
    nothing = jnp.zeros(mixed.shape, jnp.bfloat16)
    upper = jnp.concatenate([mixed, nothing], axis=1)
    lower = jnp.concatenate([nothing, mixed], axis=1)
    return dot(jnp.concatenate([upper, lower], axis=0), choice).T.astype(jnp.bfloat16)


def first_mix_kernel(top_count, received_ref, temporal_ref, others_ref, out_ref, choice_ref, other_rows_ref):
    block_count = others_ref.shape[1]
    square = (block_count, block_count)
    on_diagonal = lax.broadcasted_iota(jnp.int32, square, 0) == lax.broadcasted_iota(
        jnp.int32, square, 1
    )
    others = jnp.where(on_diagonal, jnp.broadcast_to(others_ref[...], square), 0)
    others = jnp.sum(others, axis=1, keepdims=True)
    other_rows_ref[...] = jnp.broadcast_to(others, other_rows_ref.shape)
    periods = temporal_ref.shape[0]
    wide = received_ref[...].astype(jnp.float32).T
    shape = (periods, wide.shape[1])
    period = lax.broadcasted_iota(jnp.int32, shape, 0).astype(jnp.float32)
    for column in range(2):
        choice = jnp.zeros(shape, jnp.float32)
        for top in range(top_count):
            at = column * HALF_LANES + GROUP + top
            weight = wide[at + top_count : at + top_count + 1]
            choice = jnp.where(wide[at : at + 1] == period, weight, choice)
        choice_ref[column * periods : (column + 1) * periods, :] = choice.astype(jnp.bfloat16)
    out_ref[...] = mix(received_ref[...], choice_ref[...], temporal_ref[...])


def mix_kernel(received_ref, temporal_ref, choice_ref, out_ref):
    out_ref[...] = mix(received_ref[...], choice_ref[...], temporal_ref[...])


def column_spans(count, width):
    ends = [0, width + width // 4, 2 * width + width // 2, count]
    return list(zip(ends[:-1], ends[1:]))


def spatial_kernel(block_count, depth, width, streamed, received_ref, tile_rows_ref, other_rows_ref, *refs):
    if streamed:
        own_in, top_in, rest_in, feet_in, out_ref, kept_ref, feet_ref, field, total, sems = refs
    else:
        kept_ref, out_ref, field, total = refs
    rows, half_cells = field.shape
    probe_count = rows // block_count
    tile_count = half_cells // LANES
    own_copies, other_copies = [], []
    if streamed:
        pairs = [
            (own_in.at[at : at + depth, at:], kept_ref.at[0, at : at + depth, at:])
            for at in range(0, half_cells, depth)
        ]
        for at, end in column_spans(half_cells, width):
            columns = slice(at, end)
            pairs.append((top_in.at[:, columns], kept_ref.at[1, :depth, columns]))
            pairs.append((rest_in.at[:, columns], kept_ref.at[1, depth:, columns]))
        pairs.append((feet_in, feet_ref))
        copies = [
            pltpu.make_async_copy(source, target, sems.at[place])
            for place, (source, target) in enumerate(pairs)
        ]
        for copy in copies:
            copy.start()
        own_copies, other_copies = copies[: half_cells // depth], copies[half_cells // depth :]
        feet_copy = copies[-1]
    size = 2 * block_count

    def unpack(probe, carry):
        into = pl.multiple_of(probe * block_count, block_count)
        for triple in range(tile_count // 3):
            at = pl.multiple_of(2 * size * (probe * (tile_count // 3) + triple), size)
            both = received_ref[pl.ds(at, 2 * size), :].astype(jnp.float32)
            packed = [both[part * block_count : (part + 1) * block_count] for part in range(4)]
            for part, value in enumerate(unpack_groups(packed)):
                start = (3 * triple + part) * LANES
                field[pl.ds(into, block_count), start : start + LANES] = value
        return carry

    if streamed:
        lax.fori_loop(0, probe_count, unpack, 0)
    else:
        for pair in range(tile_count * probe_count // 2):
            both = received_ref[size * pair : size * (pair + 1), :].astype(jnp.float32)
            for part in range(2):
                tile, probe = divmod(2 * pair + part, probe_count)
                field[
                    probe * block_count : (probe + 1) * block_count,
                    tile * LANES : (tile + 1) * LANES,
                ] = swap_quarters(both[part * block_count : (part + 1) * block_count])
    cells = field[...].astype(jnp.bfloat16)
    for copy in own_copies:
        copy.wait()
    for at in range(0, half_cells, depth):
        end = at + depth
        value = dot(cells[:, :end], kept_ref[0, :end, at:end])
        if end < half_cells:
            value = value + dot(cells[:, end:], kept_ref[0, at:end, end:], ((1,), (1,)))
        total[:, at:end] = value
    for place, (at, end) in enumerate(column_spans(half_cells, width)):
        for copy in other_copies[2 * place : 2 * place + 2]:
            copy.wait()
        total[:, half_cells + at : half_cells + end] = dot(cells, kept_ref[1, :, at:end])
    nothing = jnp.zeros((block_count, LANES), jnp.float32)
    for side, rows_ref in enumerate((tile_rows_ref, other_rows_ref)):
        first_tile = rows_ref[...]
        for probe in range(probe_count):
            rows_of = slice(probe * block_count, (probe + 1) * block_count)
            window = [nothing, nothing]
            for tile in range(tile_count):
                at = side * half_cells + tile * LANES
                values = total[rows_of, at : at + LANES]
                for part in range(2):
                    window[part] = jnp.where(first_tile == tile - part, values, window[part])
            for part in range(2):
                at = (2 * side + part) * LANES
                out_ref[rows_of, at : at + LANES] = window[part]
    if streamed:
        feet_copy.wait()


def sound(mine_ref, theirs_ref, feet_ref, other_feet_ref):
    block_count, sound_count, window = feet_ref.shape
    rows = mine_ref.shape[0]
    own = (mine_ref[:, :window] + theirs_ref[:, window:]).astype(jnp.bfloat16)
    other = (mine_ref[:, window:] + theirs_ref[:, :window]).astype(jnp.bfloat16)
    block_index = block_of_row((rows, sound_count), block_count)
    image = jnp.zeros((rows, sound_count), jnp.float32)
    for block in range(block_count):
        part = dot(own, feet_ref[block], ((1,), (1,)))
        part = part + dot(other, other_feet_ref[block], ((1,), (1,)))
        image = jnp.where(block_index == block, part, image)
    return image


def turn_kernel(mine_ref, theirs_ref, feet_ref, other_feet_ref, tile_rows_ref, out_ref, image_ref):
    image = sound(mine_ref, theirs_ref, feet_ref, other_feet_ref)
    image_ref[...] = image
    pieces = adjoint_pieces(image.astype(jnp.bfloat16), feet_ref)
    tile_rows = tile_rows_ref[...]
    size = 2 * feet_ref.shape[0]
    probe_count = image.shape[0] // feet_ref.shape[0]
    count = out_ref.shape[0] // size * 3 // 4
    for pair in range(count):
        tiles = [
            swap_quarters(
                placed_tile(pieces, tile_rows, *divmod(2 * pair + part, probe_count), probe_count)
            )
            for part in range(2)
        ]
        out_ref[size * pair : size * (pair + 1), :] = jnp.concatenate(tiles, axis=0).astype(
            jnp.bfloat16
        )
    out_ref[size * count :, :] = jnp.zeros((out_ref.shape[0] - size * count, LANES), jnp.bfloat16)


def last_kernel(probe_count, mine_ref, theirs_ref, feet_ref, other_feet_ref, probes_ref, first_ref, sums_ref, second_ref):
    second = sound(mine_ref, theirs_ref, feet_ref, other_feet_ref)
    second_ref[...] = second
    probes = probes_ref[...]
    first = first_ref[...]
    block_count = second.shape[0] // probe_count
    lane = lax.broadcasted_iota(jnp.int32, (1, LANES), 1)
    row = jnp.zeros((1, LANES), jnp.float32)
    pairs = (
        (probes, probes),
        (probes, first),
        (first, first),
        (probes, second),
        (first, second),
        (second, second),
    )
    for place, (left, right) in enumerate(pairs):
        product = left * right
        for probe in range(probe_count):
            value = jnp.sum(
                product[probe * block_count : (probe + 1) * block_count], axis=0, keepdims=True
            )
            value = jnp.sum(value, axis=1, keepdims=True)
            row = jnp.where(lane == place * probe_count + probe, value, row)
    sums_ref[...] = jnp.broadcast_to(row, sums_ref.shape)


def finish_kernel(total_rows, sums_ref, probes_ref, first_ref, second_ref, coefficients_ref, residual_ref):
    block_count, probe_count, half_sound = residual_ref.shape
    row = jnp.sum(sums_ref[...], axis=0, keepdims=True) / total_rows

    def stat(place):
        shift = (LANES - place * probe_count) % LANES
        return row if shift == 0 else pltpu.roll(row, shift, 1)

    pp, pw, ww, px, wx, xx = [stat(place) for place in range(6)]
    scale_square = pp + epsilon
    scale = jnp.sqrt(scale_square)
    alpha_one = pw / scale_square
    rest = (ww - 2.0 * alpha_one * pw + alpha_one * alpha_one * pp) / scale_square
    beta_one = jnp.sqrt(jnp.maximum(rest, 0.0) + epsilon)
    cross = wx - alpha_one * ww - alpha_one * px + alpha_one * alpha_one * pw
    alpha_two = (cross / (beta_one * beta_one) - (pw - alpha_one * pp)) / scale_square
    of_second = 1.0 / (scale * beta_one)
    of_first = -(alpha_one + alpha_two) * of_second
    of_probes = (alpha_one * alpha_two / beta_one - beta_one) / scale
    square = (
        of_second * of_second * xx
        + of_first * of_first * ww
        + of_probes * of_probes * pp
        + 2.0 * (of_second * of_first * wx + of_second * of_probes * px + of_first * of_probes * pw)
    )
    beta_two = jnp.sqrt(jnp.maximum(square, 0.0) + epsilon)
    for place, value in enumerate((alpha_one, beta_one, alpha_two, beta_two)):
        coefficients_ref[place : place + 1, :] = value[:, :probe_count]
    at = pl.multiple_of(lax.axis_index("half") * half_sound, LANES)
    for probe in range(probe_count):
        rows = slice(probe * block_count, (probe + 1) * block_count)
        residual_ref[:, probe, :] = (
            of_second[:, probe : probe + 1] * second_ref[rows, pl.ds(at, half_sound)]
            + of_first[:, probe : probe + 1] * first_ref[rows, pl.ds(at, half_sound)]
            + of_probes[:, probe : probe + 1] * probes_ref[rows, pl.ds(at, half_sound)]
        )


def body(probes, footprints, lag_weights, owners, window_tiles, coords, temporal):
    periods = lax.axis_size("period")
    block_count, top_count = owners.shape
    probe_count = probes.shape[1]
    sound_count = footprints.shape[1]
    window = footprints.shape[2]
    cell_count = coords.shape[1]
    half_cells = cell_count // 2
    rows = block_count * probe_count
    total_rows = float(block_count * periods * sound_count)
    f32, bf16 = jnp.float32, jnp.bfloat16
    wire = pltpu.VMEM((periods * HALF_SUBLANES, LANES), bf16)
    vectors = pltpu.VMEM((rows, sound_count), f32)

    def call(kernel, scalars, values, outputs, scratch=(), left_in_hbm=()):
        outputs = tuple(outputs)
        results = pl.pallas_call(
            kernel,
            out_shape=outputs,
            in_specs=[smem] * len(scalars) + [vmem] * len(values) + [hbm] * len(left_in_hbm),
            out_specs=tuple(vmem for _ in outputs),
            scratch_shapes=list(scratch),
            compiler_params=small,
        )(
            *scalars,
            *[in_vmem(value) for value in values],
            *[in_hbm(value) for value in left_in_hbm],
        )
        return results if len(outputs) > 1 else results[0]

    def send(value):
        count = value.shape[0] // periods
        return exchange(value.reshape(periods, count, LANES)).reshape(value.shape)

    depth, width = 256, 512
    block_rows = half_cells // depth

    def first_build():
        return pl.pallas_call(
            first_build_kernel,
            out_shape=(
                pltpu.HBM((half_cells, half_cells), bf16),
                pltpu.HBM((depth, half_cells), bf16),
            ),
            in_specs=[vmem, vmem],
            out_specs=(hbm, hbm),
            scratch_shapes=[
                pltpu.VMEM((block_rows + 1, depth, half_cells), bf16),
                pltpu.SemaphoreType.DMA((block_rows + 1,)),
            ],
            compiler_params=small,
            name="first_build",
        )(in_vmem(left), in_vmem(right))

    def second_build():
        return pl.pallas_call(
            second_build_kernel,
            out_shape=pltpu.HBM((half_cells - depth, half_cells), bf16),
            in_specs=[vmem, vmem],
            out_specs=hbm,
            scratch_shapes=[
                pltpu.VMEM((block_rows - 1, depth, half_cells), bf16),
                pltpu.SemaphoreType.DMA((block_rows - 1,)),
            ],
            compiler_params=small,
            name="second_build",
        )(in_vmem(left), in_vmem(right))

    def spatial_step(received, kept):
        scratch = [pltpu.VMEM((rows, half_cells), f32), pltpu.VMEM((rows, cell_count), f32)]
        outputs = [pltpu.VMEM((rows, 2 * window), f32)]
        values, stored = (received, tile_rows, other_rows), ()
        if kept is None:
            outputs.append(pltpu.VMEM((2, half_cells, half_cells), bf16))
            outputs.append(pltpu.VMEM(footprints.shape, bf16))
            count = block_rows + 2 * half_cells // width + 1
            scratch.append(pltpu.SemaphoreType.DMA((count,)))
            stored = (own_spatial, top_spatial, rest_spatial, other_feet)
        else:
            values = values + (kept,)
        results = call(
            functools.partial(spatial_kernel, block_count, depth, width, kept is None),
            (),
            values,
            outputs,
            scratch,
            stored,
        )
        if kept is None:
            mine, kept, feet = results
            return mine, from_other_half(mine), kept, feet
        return results, from_other_half(results)

    tiles = window_tiles.reshape(-1)
    other_probes = from_other_half(probes)
    own_probes, table, tile_rows, left, right, first_feet = call(
        prepare_kernel,
        (),
        (),
        (
            pltpu.VMEM((rows, sound_count // 2), f32),
            pltpu.VMEM((2 * HALF_SUBLANES, LANES), f32),
            pltpu.VMEM((2 * HALF_SUBLANES, LANES), jnp.int32),
            pltpu.VMEM((16, half_cells), bf16),
            pltpu.VMEM((16, cell_count), bf16),
            pltpu.VMEM(footprints.shape, bf16),
        ),
        (
            pltpu.SMEM(tiles.shape, jnp.int32),
            pltpu.SMEM((top_count, block_count), jnp.int32),
            pltpu.SMEM((top_count, block_count), f32),
            pltpu.VMEM(probes.shape, f32),
            pltpu.VMEM(coords.shape, jnp.int32),
            pltpu.SemaphoreType.DMA((6,)),
        ),
        (tiles, owners.T, lag_weights.T, probes, coords, footprints),
    )
    to_mix, all_probes = call(
        start_kernel, (), (own_probes, other_probes, table, tile_rows, first_feet), (wire, vectors)
    )
    received = send(to_mix)
    other_feet = from_other_half(footprints)
    other_tiles = from_other_half(tiles)
    own_spatial, top_spatial = first_build()
    received, own_spatial, top_spatial = lax.optimization_barrier(
        (received, own_spatial, top_spatial)
    )
    mixed, choice, other_rows = call(
        functools.partial(first_mix_kernel, top_count),
        (),
        (received, temporal, other_tiles.reshape(1, -1)),
        (
            wire,
            pltpu.VMEM((2 * periods, periods * HALF_SUBLANES), bf16),
            pltpu.VMEM((block_count, LANES), jnp.int32),
        ),
    )
    rest_spatial = second_build()
    mine, theirs, kept, other_feet = spatial_step(send(mixed), None)
    to_mix, first = call(
        turn_kernel, (), (mine, theirs, footprints, other_feet, tile_rows), (wire, vectors)
    )
    mixed = call(mix_kernel, (), (send(to_mix), temporal, choice), (wire,))
    mine, theirs = spatial_step(send(mixed), kept)
    sums, second = call(
        functools.partial(last_kernel, probe_count),
        (),
        (mine, theirs, footprints, other_feet, all_probes, first),
        (pltpu.VMEM((periods, LANES), f32), vectors),
    )
    sums = exchange(sums.reshape(periods, 1, LANES)).reshape(periods, LANES)
    return pl.pallas_call(
        functools.partial(finish_kernel, total_rows),
        out_shape=(
            jax.ShapeDtypeStruct((4, probe_count), f32),
            jax.ShapeDtypeStruct(probes.shape, f32),
        ),
        in_specs=[vmem, vmem, vmem, vmem],
        out_specs=(vmem, vmem),
        compiler_params=small,
        name="finish",
    )(in_vmem(sums), in_vmem(all_probes), in_vmem(first), in_vmem(second))


def solution(mesh):
    in_specs = (
        P("period", None, "half"),
        P("period", None, "half"),
        P("period", None),
        P("period", None),
        P("period", "half"),
        P(),
        P(),
    )
    out_specs = (P(), P("period", None, "half"))
    return jax.shard_map(body, mesh=mesh, in_specs=in_specs, out_specs=out_specs, check_vma=False)
```
